32 devices in a mesh: ma: 16 (over z, y, x), ch: 2 (over core).
Axes of the slice: x: 2, y: 2, z: 4, core: 2. Of those that a mesh axis runs over, the one named last changes fastest.
Arguments:
- visibilities: bfloat16 [512, 512, 2, 128], P('ma', 'ch'), may hold values from -6 to 6
- kl_basis: bfloat16 [512, 256, 2, 512], P('ma', 'ch'), may hold values from -0.1875 to 0.1875
- time_flags: int32 [512], P('ma'), may hold values 0 or 1
Outputs:
- kl_modes: bfloat16 [512, 256, 2, 128], P('ma', 'ch')
The draws below stay inside these ranges and needn't reach their ends.
All inputs are finite; a program needn't handle non-finite values. No bound on the sum of `time_flags` on one device may be relied on, other than what follows from the above.
Results may differ from the reference program's by a relative error of at most 0.006.
Values may be sent and summed in bfloat16 or wider, within the bound.
No kernel may reach another device: no remote copies, remote signals or barrier semaphores. Data moves between devices by JAX's collectives and lax.ppermute only.
A program may use at most 128 MiB of HBM per device.

```python
import math
import jax
import jax.numpy as jnp
from jax import lax

C = 512
KL = 256
S = 128
H = 128
M = 512


def with_ends(values, rng, smallest, high):
    dims = values.shape
    spot = [jax.random.randint(jax.random.fold_in(rng, axis), (), 0, dims[axis]) for axis in range(len(dims))]
    values = values.at[tuple(spot)].set(smallest)
    longest = dims.index(max(dims))
    spot[longest] = (spot[longest] + 1) % dims[longest]
    return values.at[tuple(spot)].set(high)


def shard_levels(key, dims, shards, least, top_value):
    def one(axis_at, blocks):
        heights = jax.random.uniform(jax.random.fold_in(jax.random.fold_in(key, 6), axis_at), (blocks,), jnp.float32, least / len(shards), top_value / len(shards))
        return jnp.repeat(jnp.exp(heights), dims[axis_at] // blocks).reshape((-1,) + (1,) * (len(dims) - axis_at - 1))

    level = one(*shards[0])
    for cut in shards[1:]:
        level = level * one(*cut)
    return level


def bell_draw(key, dims, deviation, bound, split=(), kind=jnp.bfloat16):
    values = jax.random.normal(key, dims, jnp.float32) * deviation
    if len(split) > 0:
        values = shard_levels(key, dims, split, -0.22, 0.18) * values
    return jnp.clip(values, min=-bound, max=bound).astype(kind)


def setup_inputs(seed: int = 0) -> dict:
    key_list = jax.random.split(jax.random.key(seed), 4)
    return {
        "visibilities": bell_draw(key_list[0], (M, C, 2, S), 1.0, 6.0, ((0, 16), (1, 2))),
        "kl_basis": bell_draw(key_list[1], (M, KL, 2, C), (2 * C) ** -0.5, 0.1875, ((0, 16), (1, 2))),
        "time_flags": with_ends((jax.random.randint(key_list[2], (M,), 0, 2) < 1).astype(jnp.int32), jax.random.fold_in(key_list[2], 1), 0, 1),
    }


def tap_table(offsets, total):
    shifts = jnp.mod(jnp.arange(2 * H + 1, dtype=jnp.int32) - H, total).astype(jnp.int32)
    phase_index = jnp.mod(shifts[:, None] * offsets[None, :], total).astype(jnp.int32)
    phases = phase_index.astype(jnp.float32) * (2.0 * math.pi / total)
    return jnp.cos(phases), jnp.sin(phases)


def toeplitz(kernel_taps, block_rows):
    width = kernel_taps.shape[1]
    span = block_rows + width - 1
    reverse = kernel_taps[:, ::-1]
    padded = jnp.concatenate([reverse, jnp.zeros((2, block_rows), kernel_taps.dtype)], axis=1)
    tiled = jnp.tile(padded, (1, block_rows))[:, :block_rows * span].reshape(2, block_rows, span)
    real_part = tiled[0]
    imag_part = tiled[1]
    first = jnp.stack([real_part, -imag_part], 1)
    second = jnp.stack([imag_part, real_part], 1)
    return jnp.stack([first, second], 0)


def reference(visibilities, kl_basis, time_flags):
    total = M
    offsets = jnp.arange(total, dtype=jnp.int32)
    cosine, sine_table = tap_table(offsets, total)
    flag_values = time_flags.astype(jnp.float32)
    real_sum = jnp.dot(cosine, flag_values, precision=lax.Precision.HIGHEST)
    imag_sum = jnp.dot(sine_table, flag_values, precision=lax.Precision.HIGHEST)
    kernel_taps = (jnp.stack([real_sum, -imag_sum]) / total).astype(jnp.bfloat16)
    block_rows = math.gcd(total, 128)
    toeplitz_block = toeplitz(kernel_taps, block_rows).astype(jnp.float32)
    extended = jnp.concatenate([visibilities[total - H:], visibilities, visibilities[:H]], axis=0)

    def convolve(block_index):
        rows = lax.dynamic_slice_in_dim(extended, block_index * block_rows, block_rows + 2 * H, 0).astype(jnp.float32)
        return jnp.einsum('pbqe,ecqs->bcps', toeplitz_block, rows).astype(jnp.bfloat16)

    blocks = lax.map(convolve, jnp.arange(total // block_rows, dtype=jnp.int32))
    mixed_rows = blocks.reshape(visibilities.shape)
    group = math.gcd(total, 32)

    def project(block_index):
        basis = lax.dynamic_slice_in_dim(kl_basis, block_index * group, group, 0).astype(jnp.float32)
        data = lax.dynamic_slice_in_dim(mixed_rows, block_index * group, group, 0).astype(jnp.float32)
        products = jnp.einsum('mkqc,mcrs->mkqrs', basis, data)
        real_out = products[:, :, 0, 0, :] - products[:, :, 1, 1, :]
        imag_out = products[:, :, 0, 1, :] + products[:, :, 1, 0, :]
        return jnp.stack([real_out, imag_out], 2).astype(jnp.bfloat16)

    results = lax.map(project, jnp.arange(total // group, dtype=jnp.int32))
    return results.reshape(total, kl_basis.shape[1], 2, visibilities.shape[3])
```

```python
import functools
import math

import jax
import jax.numpy as jnp
from jax import lax
from jax.experimental import pallas as pl
from jax.experimental.pallas import tpu as pltpu
from jax.sharding import PartitionSpec as P

H = 128
PARTS = (3, 3, 1, 1)


def regroup(position, visibilities, picks, width):
    rows, _, two, svd = visibilities.shape

    def kernel(pos_ref, src, *refs):
        outs = refs[: len(picks)]
        buf, load_sem, store_sem = refs[len(picks) :]
        loads = []
        for n, pick in enumerate(picks):
            start = lax.bitwise_xor(pos_ref[0], pick) * width
            for m in range(rows):
                loads.append(
                    pltpu.make_async_copy(src.at[m, pl.ds(start, width)], buf.at[n, :, m], load_sem.at[n, m])
                )
        for copy in loads:
            copy.start()
        stores = []
        for n in range(len(picks)):
            for m in range(rows):
                loads[n * rows + m].wait()
            stores.append(pltpu.make_async_copy(buf.at[n], outs[n], store_sem.at[n]))
            stores[-1].start()
        for copy in stores:
            copy.wait()

    shape = (width, rows, two, svd)
    nbytes = 4 * len(picks) * math.prod(shape)
    outs = pl.pallas_call(
        kernel,
        out_shape=[jax.ShapeDtypeStruct(shape, visibilities.dtype)] * len(picks),
        in_specs=[pl.BlockSpec(memory_space=pltpu.SMEM), pl.BlockSpec(memory_space=pl.ANY)],
        out_specs=[pl.BlockSpec(memory_space=pl.ANY)] * len(picks),
        scratch_shapes=[
            pltpu.VMEM((len(picks),) + shape, visibilities.dtype),
            pltpu.SemaphoreType.DMA((len(picks), rows)),
            pltpu.SemaphoreType.DMA((len(picks),)),
        ],
        cost_estimate=pl.CostEstimate(flops=0, bytes_accessed=nbytes, transcendentals=0),
        name="regroup",
    )(position, visibilities)
    return [out.reshape(width, rows * two, svd) for out in outs]


def mixing_matrix(flag_values, out_rows, in_rows, total):
    t = jnp.arange(total, dtype=jnp.int32)

    def waves(rows):
        index = jnp.mod(rows[:, None] * t[None, :], total)
        phases = index.astype(jnp.float32) * (2.0 * math.pi / total)
        return jnp.cos(phases), jnp.sin(phases)

    co, so = waves(out_rows)
    ci, si = waves(in_rows)
    ci, si = ci * flag_values, si * flag_values
    left = jnp.stack([jnp.concatenate([co, so], 1), jnp.concatenate([-so, co], 1)], 1)
    right = jnp.stack([jnp.concatenate([ci, si], 1), jnp.concatenate([-si, ci], 1)], 1)
    left = left.reshape(-1, 2 * total)
    right = right.reshape(-1, 2 * total)
    taps = lax.dot_general(left, right, (((1,), (1,)), ((), ())), precision=lax.Precision.HIGHEST) / total
    distance = jnp.repeat(out_rows, 2)[:, None] - jnp.repeat(in_rows, 2)[None, :]
    return jnp.where(jnp.abs(distance) <= H, taps, 0.0).astype(jnp.bfloat16)


def mix(matrix, firsts, others, offset, unit, size):
    pair_rows, svd = firsts[0].shape[1:]
    group = others[0].shape[0] + 1
    rows = pair_rows // 2
    start = offset // unit

    def kernel(t_ref, f0, f1, f2, o0, o1, o2, *outs):
        matrix = t_ref[...]
        for c in range(0, unit, 2):
            stack = []
            for f, o in ((f0, o0), (f1, o1), (f2, o2)):
                stack.append(jnp.concatenate([f[c], f[c + 1]], axis=1))
                for p in range(group - 1):
                    stack.append(jnp.concatenate([o[p, c], o[p, c + 1]], axis=1))
            mixed = jnp.dot(matrix, jnp.concatenate(stack, axis=0), preferred_element_type=jnp.float32)
            mixed = mixed.astype(jnp.bfloat16)
            for r in range(group):
                part = mixed[r * pair_rows : (r + 1) * pair_rows]
                outs[r][:, c] = part[:, :svd].reshape(rows, 2, svd)
                outs[r][:, c + 1] = part[:, svd:].reshape(rows, 2, svd)

    first_spec = pl.BlockSpec((unit, pair_rows, svd), lambda i: (start + i, 0, 0))
    other_spec = pl.BlockSpec((group - 1, unit, pair_rows, svd), lambda i: (0, i, 0, 0))
    out_spec = pl.BlockSpec((rows, unit, 2, svd), lambda i: (0, i, 0, 0))
    flops = 2 * matrix.shape[0] * matrix.shape[1] * size * svd
    nbytes = 2 * (matrix.size + (3 + 1) * group * size * pair_rows * svd)
    return pl.pallas_call(
        kernel,
        grid=(size // unit,),
        out_shape=[jax.ShapeDtypeStruct((rows, size, 2, svd), jnp.bfloat16)] * group,
        in_specs=[pl.BlockSpec(matrix.shape, lambda i: (0, 0))] + [first_spec] * 3 + [other_spec] * 3,
        out_specs=[out_spec] * group,
        cost_estimate=pl.CostEstimate(flops=flops, bytes_accessed=nbytes, transcendentals=0),
        name="mix",
    )(matrix, *firsts, *others)


def arrange_basis(kl_basis, selectors):
    rows, modes, two, chans = kl_basis.shape
    widths = [s.shape[1] for s, _ in selectors]

    def kernel(kl_ref, *refs):
        sel = refs[: 2 * len(widths)]
        outs = refs[2 * len(widths) :]
        plain = kl_ref[0].reshape(2 * modes, chans)
        r = lax.broadcasted_iota(jnp.int32, (2 * modes, 2 * modes), 0)
        c = lax.broadcasted_iota(jnp.int32, (2 * modes, 2 * modes), 1)
        odd = lax.rem(r, 2) == 1
        turn = jnp.where(c == jnp.where(odd, r - 1, r + 1), jnp.where(odd, 1.0, -1.0), 0.0).astype(jnp.bfloat16)
        turned = jnp.dot(turn, plain, preferred_element_type=jnp.float32).astype(jnp.bfloat16)
        for n in range(len(widths)):
            value = jnp.dot(plain, sel[2 * n][...], preferred_element_type=jnp.float32)
            value += jnp.dot(turned, sel[2 * n + 1][...], preferred_element_type=jnp.float32)
            outs[n][0] = value.astype(jnp.bfloat16)

    flat = [s for pair in selectors for s in pair]
    flops = 4 * rows * 2 * modes * chans * sum(widths)
    nbytes = 2 * (kl_basis.size + rows * 2 * modes * sum(widths))
    return pl.pallas_call(
        kernel,
        grid=(rows,),
        out_shape=[jax.ShapeDtypeStruct((rows, 2 * modes, w), jnp.bfloat16) for w in widths],
        in_specs=[pl.BlockSpec((1, modes, two, chans), lambda i: (i, 0, 0, 0))]
        + [pl.BlockSpec(s.shape, lambda i: (0, 0)) for s in flat],
        out_specs=[pl.BlockSpec((1, 2 * modes, w), lambda i: (i, 0, 0)) for w in widths],
        cost_estimate=pl.CostEstimate(flops=flops, bytes_accessed=nbytes, transcendentals=0),
        name="arrange",
    )(kl_basis, *flat)


def project(basis, pieces, total, last):
    rows, out_rows, width = basis.shape
    svd = pieces[0].shape[2]
    if pieces[0].shape[1] % 16 != 0:
        pieces = [jnp.concatenate(pieces, axis=1)]
    step = math.gcd(rows, 4)
    has_total = total is not None

    def kernel(a_ref, *refs):
        out = refs[-1]
        for m in range(step):
            data = jnp.concatenate([ref[m] for ref in refs[: len(pieces)]], axis=0)
            value = jnp.dot(a_ref[m], data, preferred_element_type=jnp.float32)
            if has_total:
                value += refs[len(pieces)][m]
            out[m] = value.astype(out.dtype)

    spec = lambda shape: pl.BlockSpec((step,) + shape, lambda i: (i, 0, 0))
    args = [basis] + list(pieces) + ([total] if has_total else [])
    dtype = jnp.bfloat16 if last else jnp.float32
    flops = 2 * rows * out_rows * width * svd
    nbytes = sum(a.size * a.dtype.itemsize for a in args) + rows * out_rows * svd * dtype.dtype.itemsize
    return pl.pallas_call(
        kernel,
        grid=(rows // step,),
        out_shape=jax.ShapeDtypeStruct((rows, out_rows, svd), dtype),
        in_specs=[spec(a.shape[1:]) for a in args],
        out_specs=spec((out_rows, svd)),
        cost_estimate=pl.CostEstimate(flops=flops, bytes_accessed=nbytes, transcendentals=0),
        name="project",
    )(*args)


def on_device(visibilities, kl_basis, time_flags):
    rows, chans, _, svd = visibilities.shape
    modes = kl_basis.shape[1]
    count = lax.axis_size("ma")
    copies = lax.axis_size("ch")
    total = rows * count
    group = H // rows
    width = chans // group
    unit = width // sum(PARTS)
    me = lax.axis_index("ma")
    core = lax.axis_index("ch")
    place = lax.rem(me, group)

    def swap(x, bits):
        return lax.ppermute(x, "ma", [(i, i ^ bits) for i in range(count)])

    def shift(x, by):
        return lax.ppermute(x, "ma", [(i, (i + by * group) % count) for i in range(count)])

    flags = lax.dynamic_update_slice(jnp.zeros((total,), jnp.int32), time_flags, (me * rows,))
    bits = count // 2
    while bits:
        flags = flags + swap(flags, bits)
        bits //= 2

    position = place.reshape(1).astype(jnp.int32)
    (own,) = regroup(position, visibilities, (0,), width)
    away = regroup(position, visibilities, tuple(range(1, group)), width)
    own_up, own_down = shift(own, 1), shift(own, -1)
    near = [swap(away[p - 1], p) for p in range(1, group)]

    order = lax.bitwise_xor(jnp.arange(group, dtype=jnp.int32), place.astype(jnp.int32))
    out_rows = (order[:, None] * rows + jnp.arange(rows, dtype=jnp.int32)[None, :]).reshape(-1)
    in_rows = jnp.concatenate([out_rows, out_rows - H, out_rows + H])
    matrix = mixing_matrix(flags.astype(jnp.float32), out_rows, in_rows, total)

    selectors = []
    offset = 0
    for part in PARTS:
        size = part * unit
        shape = (copies, group, size, 2)
        source = lax.rem(core + lax.broadcasted_iota(jnp.int32, shape, 0), copies)
        quarter = lax.bitwise_xor(lax.broadcasted_iota(jnp.int32, shape, 1), place.astype(jnp.int32))
        channel = source * chans + quarter * width + offset + lax.broadcasted_iota(jnp.int32, shape, 2)
        plane = lax.broadcasted_iota(jnp.int32, shape, 3).reshape(-1)
        hit = channel.reshape(1, -1) == jnp.arange(copies * chans, dtype=jnp.int32)[:, None]
        selectors.append(tuple((hit & (plane == v)[None, :]).astype(jnp.bfloat16) for v in (0, 1)))
        offset += size
    bases = arrange_basis(kl_basis, selectors)

    result = None
    offset = 0
    for n, part in enumerate(PARTS):
        size = part * unit
        here = jnp.stack([piece[offset : offset + size] for piece in near], 0)
        up, down = shift(here, 1), shift(here, -1)
        mixed = mix(matrix, (own, own_up, own_down), (here, up, down), offset, unit, size)
        back = [mixed[0]] + [swap(mixed[p], p) for p in range(1, group)]
        held = []
        for o in range(copies):
            for piece in back:
                if o:
                    piece = lax.ppermute(piece, "ch", [(i, (i - o) % copies) for i in range(copies)])
                held.append(piece.reshape(rows, size * 2, svd))
        result = project(bases[n], held, result, n == len(PARTS) - 1)
        offset += size
    return result.reshape(rows, modes, 2, svd)


def solution(mesh):
    return jax.shard_map(
        on_device,
        mesh=mesh,
        in_specs=(P("ma", "ch", None, None), P("ma", "ch", None, None), P("ma")),
        out_specs=P("ma", "ch", None, None),
        check_vma=False,
    )
```

```python
import functools
import math

import jax
import jax.numpy as jnp
from jax import lax
from jax.experimental import pallas as pl
from jax.experimental.pallas import tpu as pltpu
from jax.sharding import PartitionSpec as P


H = 128
UNITS = 8
SPANS = (4, 2, 2)
PARTS = (4, 2, 1, 1)
JOINED = ((0,), (1,), (2, 3))
VMEM_BYTES = 24 << 20


def regroup(position, visibilities, picks, width):
    rows, _, two, svd = visibilities.shape
    shapes = [(size, rows, two, svd) for _, _, size in picks]

    def kernel(pos_ref, src, *refs):
        outs, bufs = refs[: len(picks)], refs[len(picks) : 2 * len(picks)]
        load_sem, store_sem = refs[2 * len(picks) :]
        for n, (partner, offset, size) in enumerate(picks):
            start = lax.bitwise_xor(pos_ref[0], partner) * width + offset

            @pl.loop(0, rows)
            def load(m):
                pltpu.make_async_copy(src.at[m, pl.ds(start, size)], bufs[n].at[:, m], load_sem.at[n]).start()

        stores = []
        for n in range(len(picks)):
            pltpu.make_async_copy(bufs[n], bufs[n], load_sem.at[n]).wait()
            stores.append(pltpu.make_async_copy(bufs[n], outs[n], store_sem.at[n]))
            stores[-1].start()
        for copy in stores:
            copy.wait()

    nbytes = 4 * sum(math.prod(shape) for shape in shapes)
    outs = pl.pallas_call(
        kernel,
        out_shape=[jax.ShapeDtypeStruct(shape, visibilities.dtype) for shape in shapes],
        in_specs=[pl.BlockSpec(memory_space=pltpu.SMEM), pl.BlockSpec(memory_space=pl.ANY)],
        out_specs=[pl.BlockSpec(memory_space=pl.ANY)] * len(picks),
        scratch_shapes=[pltpu.VMEM(shape, visibilities.dtype) for shape in shapes]
        + [pltpu.SemaphoreType.DMA((len(picks),)), pltpu.SemaphoreType.DMA((len(picks),))],
        compiler_params=pltpu.CompilerParams(vmem_limit_bytes=VMEM_BYTES),
        cost_estimate=pl.CostEstimate(flops=0, bytes_accessed=nbytes, transcendentals=0),
        name="regroup",
    )(position, visibilities)
    return [out.reshape(out.shape[0], rows * two, svd) for out in outs]


def mixing_matrix(flag_values, out_rows, in_rows, total):
    t = jnp.arange(total, dtype=jnp.int32)

    def waves(rows):
        turn = (total // 4) * jnp.tile(jnp.arange(2, dtype=jnp.int32), rows.shape[0])
        index = jnp.mod(jnp.repeat(rows, 2)[:, None] * t[None, :] + turn[:, None], total)
        phases = index.astype(jnp.float32) * (2.0 * math.pi / total)
        return jnp.cos(phases), jnp.sin(phases)

    co, so = waves(out_rows)
    ci, si = waves(in_rows)
    dot = functools.partial(
        lax.dot_general, dimension_numbers=(((1,), (1,)), ((), ())), precision=lax.Precision.HIGHEST
    )
    taps = (dot(co * flag_values, ci) + dot(so * flag_values, si)) / total
    distance = jnp.repeat(out_rows, 2)[:, None] - jnp.repeat(in_rows, 2)[None, :]
    return jnp.where(jnp.abs(distance) <= H, taps, 0.0).astype(jnp.bfloat16)


def mix(matrix, pieces, unit, size):
    pair_rows, svd = pieces[0][0].shape[1:]
    group = matrix.shape[0] // pair_rows
    rows = pair_rows // 2

    def kernel(t_ref, *refs):
        ins, outs = refs[: len(pieces)], refs[len(pieces) :]
        table = t_ref[...]
        for c in range(0, unit, 2):
            data = jnp.concatenate([jnp.concatenate([ref[c], ref[c + 1]], axis=1) for ref in ins], axis=0)
            mixed = jnp.dot(table, data, preferred_element_type=jnp.float32).astype(jnp.bfloat16)
            for r in range(group):
                part = mixed[r * pair_rows : (r + 1) * pair_rows]
                outs[r][:, c] = part[:, :svd].reshape(rows, 2, svd)
                outs[r][:, c + 1] = part[:, svd:].reshape(rows, 2, svd)

    def piece_spec(offset):
        start = offset // unit
        return pl.BlockSpec((unit, pair_rows, svd), lambda i: (start + i, 0, 0))

    flops = 2 * matrix.shape[0] * matrix.shape[1] * size * svd
    nbytes = 2 * (matrix.size + (len(pieces) + group) * size * pair_rows * svd)
    return pl.pallas_call(
        kernel,
        grid=(size // unit,),
        out_shape=[jax.ShapeDtypeStruct((rows, size, 2, svd), jnp.bfloat16)] * group,
        in_specs=[pl.BlockSpec(matrix.shape, lambda i: (0, 0))] + [piece_spec(offset) for _, offset in pieces],
        out_specs=[pl.BlockSpec((rows, unit, 2, svd), lambda i: (0, i, 0, 0))] * group,
        compiler_params=pltpu.CompilerParams(vmem_limit_bytes=VMEM_BYTES),
        cost_estimate=pl.CostEstimate(flops=flops, bytes_accessed=nbytes, transcendentals=0),
        name="mix",
    )(matrix, *[array for array, _ in pieces])


def arrange_basis(kl_basis, selectors):
    rows, modes, two, chans = kl_basis.shape
    widths = [s.shape[1] for s, _ in selectors]

    def kernel(kl_ref, *refs):
        sel = refs[: 2 * len(widths)]
        outs = refs[2 * len(widths) :]
        plain = kl_ref[0].reshape(2 * modes, chans)
        r = lax.broadcasted_iota(jnp.int32, (2 * modes, 2 * modes), 0)
        c = lax.broadcasted_iota(jnp.int32, (2 * modes, 2 * modes), 1)
        odd = lax.rem(r, 2) == 1
        turn = jnp.where(c == jnp.where(odd, r - 1, r + 1), jnp.where(odd, 1.0, -1.0), 0.0).astype(jnp.bfloat16)
        turned = jnp.dot(turn, plain, preferred_element_type=jnp.float32).astype(jnp.bfloat16)
        for n in range(len(widths)):
            value = jnp.dot(plain, sel[2 * n][...], preferred_element_type=jnp.float32)
            value += jnp.dot(turned, sel[2 * n + 1][...], preferred_element_type=jnp.float32)
            outs[n][0] = value.astype(jnp.bfloat16)

    flat = [s for pair in selectors for s in pair]
    flops = 4 * rows * 2 * modes * chans * sum(widths)
    nbytes = 2 * (kl_basis.size + rows * 2 * modes * sum(widths))
    return pl.pallas_call(
        kernel,
        grid=(rows,),
        out_shape=[jax.ShapeDtypeStruct((rows, 2 * modes, w), jnp.bfloat16) for w in widths],
        in_specs=[pl.BlockSpec((1, modes, two, chans), lambda i: (i, 0, 0, 0))]
        + [pl.BlockSpec(s.shape, lambda i: (0, 0)) for s in flat],
        out_specs=[pl.BlockSpec((1, 2 * modes, w), lambda i: (i, 0, 0)) for w in widths],
        compiler_params=pltpu.CompilerParams(vmem_limit_bytes=VMEM_BYTES),
        cost_estimate=pl.CostEstimate(flops=flops, bytes_accessed=nbytes, transcendentals=0),
        name="arrange",
    )(kl_basis, *flat)


def project(terms, total, last):
    rows, out_rows, _ = terms[0][0].shape
    svd = terms[0][1][0].shape[2]
    step = math.gcd(rows, 4)
    args, counts, flops = [], [], 0
    for basis, pieces in terms:
        if pieces[0].shape[1] % 16 != 0:
            pieces = [jnp.concatenate(pieces, axis=1)]
        args += [basis] + list(pieces)
        counts.append(len(pieces))
        flops += 2 * basis.size * svd
    has_total = total is not None
    args += [total] if has_total else []

    def kernel(*refs):
        out = refs[-1]
        for m in range(step):
            value = refs[len(args) - 1][m] if has_total else None
            at = 0
            for n in counts:
                data = jnp.concatenate([ref[m] for ref in refs[at + 1 : at + 1 + n]], axis=0)
                term = jnp.dot(refs[at][m], data, preferred_element_type=jnp.float32)
                value = term if value is None else value + term
                at += 1 + n
            out[m] = value.astype(out.dtype)

    def spec(shape):
        return pl.BlockSpec((step,) + shape, lambda i: (i, 0, 0))

    out_shape = jax.ShapeDtypeStruct((rows, out_rows, svd), jnp.bfloat16 if last else jnp.float32)
    nbytes = sum(a.size * a.dtype.itemsize for a in args) + out_shape.size * out_shape.dtype.itemsize
    return pl.pallas_call(
        kernel,
        grid=(rows // step,),
        out_shape=out_shape,
        in_specs=[spec(a.shape[1:]) for a in args],
        out_specs=spec((out_rows, svd)),
        compiler_params=pltpu.CompilerParams(vmem_limit_bytes=VMEM_BYTES),
        cost_estimate=pl.CostEstimate(flops=flops, bytes_accessed=nbytes, transcendentals=0),
        name="project",
    )(*args)


def stages(visibilities, kl_basis, time_flags):
    rows, chans, _, svd = visibilities.shape
    modes = kl_basis.shape[1]
    count = lax.axis_size("ma")
    copies = lax.axis_size("ch")
    total = rows * count
    group = H // rows
    width = chans // group
    unit = width // UNITS
    me = lax.axis_index("ma")
    core = lax.axis_index("ch")
    place = lax.rem(me, group).astype(jnp.int32)

    def swap(x, bits):
        return lax.ppermute(x, "ma", [(i, i ^ bits) for i in range(count)])

    def shift(x, by):
        return lax.ppermute(x, "ma", [(i, (i + by * group) % count) for i in range(count)])

    def both(x):
        up = shift(x, 1)
        down = shift(x, -1)
        return x, up, down

    def ranges(parts):
        starts = [sum(parts[:n]) * unit for n in range(len(parts))]
        return [(start, part * unit) for start, part in zip(starts, parts)]

    spans, chunks = ranges(SPANS), ranges(PARTS)

    position = place.reshape(1)
    (own,) = regroup(position, visibilities, ((0, 0, width),), width)
    own3 = both(own)
    picks = []
    for start, size in spans:
        picks += [(p, start, size) for p in range(1, group - 1)]
        picks += [(group - 1, s, n) for s, n in chunks if start <= s < start + size]
    away = regroup(position, visibilities, tuple(picks), width)

    mine = lax.dynamic_update_slice(jnp.zeros((total,), jnp.int32), time_flags, (me * rows,))
    flags = mine
    for by in range(1, count // group):
        flags = flags + shift(mine, by)

    held = {}
    for (p, start, size), array in zip(picks, away):
        near = swap(array, p)
        held[p, start] = both(near)

    bits = group // 2
    while bits:
        flags = flags + swap(flags, bits)
        bits //= 2

    order = lax.bitwise_xor(jnp.arange(group, dtype=jnp.int32), place)
    out_rows = (order[:, None] * rows + jnp.arange(rows, dtype=jnp.int32)[None, :]).reshape(-1)
    in_rows = jnp.concatenate([out_rows, out_rows - H, out_rows + H])
    matrix = mixing_matrix(flags.astype(jnp.float32), out_rows, in_rows, total)

    selectors = []
    for offset, size in chunks:
        shape = (copies, group, size, 2)
        source = lax.rem(core + lax.broadcasted_iota(jnp.int32, shape, 0), copies)
        quarter = lax.bitwise_xor(lax.broadcasted_iota(jnp.int32, shape, 1), place)
        channel = source * chans + quarter * width + offset + lax.broadcasted_iota(jnp.int32, shape, 2)
        plane = lax.broadcasted_iota(jnp.int32, shape, 3).reshape(-1)
        hit = channel.reshape(1, -1) == jnp.arange(copies * chans, dtype=jnp.int32)[:, None]
        selectors.append(tuple((hit & (plane == v)[None, :]).astype(jnp.bfloat16) for v in (0, 1)))
    bases = arrange_basis(kl_basis, selectors)

    spreads = []
    for offset, size in chunks:
        pieces = []
        for side in range(3):
            pieces.append((own3[side], offset))
            for p in range(1, group - 1):
                (start,) = [s for s, length in spans if s <= offset < s + length]
                pieces.append((held[p, start][side], offset - start))
            pieces.append((held[group - 1, offset][side], 0))
        mixed = mix(matrix, pieces, unit, size)
        back = [mixed[0]]
        for p in range(1, group):
            back.append(swap(mixed[p], p))
        spread = []
        for o in range(copies):
            for piece in back:
                if o:
                    piece = lax.ppermute(piece, "ch", [(i, (i - o) % copies) for i in range(copies)])
                spread.append(piece.reshape(rows, size * 2, svd))
        spreads.append(spread)

    result = None
    for n, joined in enumerate(JOINED):
        terms = [(bases[j], spreads[j]) for j in joined]
        result = project(terms, result, n == len(JOINED) - 1)
    return result.reshape(rows, modes, 2, svd)


def solution(mesh):
    return jax.shard_map(
        stages,
        mesh=mesh,
        in_specs=(P("ma", "ch", None, None), P("ma", "ch", None, None), P("ma")),
        out_specs=P("ma", "ch", None, None),
        check_vma=False,
    )
```

```python
import functools
import math

import jax
import jax.numpy as jnp
from jax import lax
from jax.experimental import pallas as pl
from jax.experimental.pallas import tpu as pltpu
from jax.sharding import PartitionSpec as P


H = 128
UNITS = 8
PARTS = (4, 2, 1, 1)
VMEM_BYTES = 24 << 20


def regroup(visibilities, picks, width, group):
    rows, _, two, svd = visibilities.shape
    shapes = [(size, rows, two, svd) for _, _, size in picks]

    def kernel(src, *refs):
        place = lax.rem(lax.axis_index("ma"), group)
        outs, bufs = refs[: len(picks)], refs[len(picks) : 2 * len(picks)]
        load_sem, store_sem = refs[2 * len(picks) :]
        for n, (partner, offset, size) in enumerate(picks):
            start = lax.bitwise_xor(place, partner) * width + offset

            @pl.loop(0, rows)
            def load(m):
                pltpu.make_async_copy(src.at[m, pl.ds(start, size)], bufs[n].at[:, m], load_sem.at[n]).start()

        stores = []
        for n in range(len(picks)):
            pltpu.make_async_copy(bufs[n], bufs[n], load_sem.at[n]).wait()
            stores.append(pltpu.make_async_copy(bufs[n], outs[n], store_sem.at[n]))
            stores[-1].start()
        for copy in stores:
            copy.wait()

    nbytes = 4 * sum(math.prod(shape) for shape in shapes)
    outs = pl.pallas_call(
        kernel,
        out_shape=[jax.ShapeDtypeStruct(shape, visibilities.dtype) for shape in shapes],
        in_specs=[pl.BlockSpec(memory_space=pltpu.HBM)],
        out_specs=[pl.BlockSpec(memory_space=pl.ANY)] * len(picks),
        scratch_shapes=[pltpu.VMEM(shape, visibilities.dtype) for shape in shapes]
        + [pltpu.SemaphoreType.DMA((len(picks),)), pltpu.SemaphoreType.DMA((len(picks),))],
        cost_estimate=pl.CostEstimate(flops=0, bytes_accessed=nbytes, transcendentals=0),
        name="regroup",
    )(visibilities)
    return [out.reshape(out.shape[0], rows * two, svd) for out in outs]


def mixing_matrix(flags, place, rows, group, total):
    def waves(count):
        at = lax.broadcasted_iota(jnp.int32, (count, total), 0)
        t = lax.broadcasted_iota(jnp.int32, (count, total), 1)
        phases = jnp.mod(row_of(at, place, rows, group) * t + (total // 4) * (at % 2), total)
        phases = phases.astype(jnp.float32) * (2.0 * math.pi / total)
        return jnp.cos(phases), jnp.sin(phases)

    outs, ins = 2 * rows * group, 6 * rows * group
    co, so, ci, si = lax.optimization_barrier(waves(outs) + waves(ins))
    kept = flags.astype(jnp.float32)
    dot = functools.partial(
        lax.dot_general, dimension_numbers=(((1,), (1,)), ((), ())), precision=lax.Precision.HIGHEST
    )
    taps = (dot(co * kept, ci) + dot(so * kept, si)) / total
    out_row = row_of(lax.broadcasted_iota(jnp.int32, taps.shape, 0), place, rows, group)
    in_row = row_of(lax.broadcasted_iota(jnp.int32, taps.shape, 1), place, rows, group)
    return jnp.where(jnp.abs(out_row - in_row) <= H, taps, 0.0).astype(jnp.bfloat16)


def row_of(at, place, rows, group):
    row = (at // 2) % rows
    block = lax.bitwise_xor((at // (2 * rows)) % group, place)
    side = at // (2 * rows * group)
    return block * rows + row + jnp.where(side == 1, -H, jnp.where(side == 2, H, 0))


def mix(matrix, firsts, others, offset, unit, size):
    pair_rows, svd = firsts[0].shape[1:]
    group = matrix.shape[0] // pair_rows
    rows = pair_rows // 2
    start = offset // unit

    def kernel(t_ref, *refs):
        ins, outs = refs[:6], refs[6:]
        table = t_ref[...]
        for c in range(0, unit, 2):
            stack = []
            for first, other in zip(ins[:3], ins[3:]):
                stack.append(jnp.concatenate([first[c], first[c + 1]], axis=1))
                for p in range(group - 1):
                    stack.append(jnp.concatenate([other[p, c], other[p, c + 1]], axis=1))
            data = jnp.concatenate(stack, axis=0)
            mixed = jnp.dot(table, data, preferred_element_type=jnp.float32).astype(jnp.bfloat16)
            for r in range(group):
                part = mixed[r * pair_rows : (r + 1) * pair_rows]
                outs[r][:, c] = part[:, :svd].reshape(rows, 2, svd)
                outs[r][:, c + 1] = part[:, svd:].reshape(rows, 2, svd)

    flops = 2 * matrix.size * size * svd
    nbytes = 2 * (matrix.size + 4 * group * size * pair_rows * svd)
    return pl.pallas_call(
        kernel,
        grid=(size // unit,),
        out_shape=[jax.ShapeDtypeStruct((rows, size, 2, svd), jnp.bfloat16)] * group,
        in_specs=[pl.BlockSpec(matrix.shape, lambda i: (0, 0))]
        + [pl.BlockSpec((unit, pair_rows, svd), lambda i: (start + i, 0, 0))] * 3
        + [pl.BlockSpec((group - 1, unit, pair_rows, svd), lambda i: (0, i, 0, 0))] * 3,
        out_specs=[pl.BlockSpec((rows, unit, 2, svd), lambda i: (0, i, 0, 0))] * group,
        compiler_params=pltpu.CompilerParams(vmem_limit_bytes=VMEM_BYTES),
        cost_estimate=pl.CostEstimate(flops=flops, bytes_accessed=nbytes, transcendentals=0),
        name="mix",
    )(matrix, *firsts, *others)


def arrange_basis(kl_basis, chunks, width, group, copies):
    rows, modes, two, chans = kl_basis.shape
    pieces = copies * group
    widths = [2 * pieces * size for _, size in chunks]

    def kernel(kl_ref, *refs):
        outs, picked = refs[: len(chunks)], refs[len(chunks) :]

        @pl.when(pl.program_id(0) == 0)
        def _():
            place = lax.rem(lax.axis_index("ma"), group)
            core = lax.axis_index("ch")
            for n, (offset, size) in enumerate(chunks):
                at = lax.broadcasted_iota(jnp.int32, (1, widths[n]), 1)
                begin = jnp.zeros_like(at)
                for piece in range(pieces):
                    source = lax.rem(core + piece // group, copies)
                    quarter = lax.bitwise_xor(place, piece % group)
                    first = source * group * width + quarter * width + offset - piece * size
                    begin = jnp.where(at >= 2 * piece * size, first, begin)
                hit = begin + (at >> 1) == lax.broadcasted_iota(jnp.int32, (chans, widths[n]), 0)
                for plane in range(2):
                    keep = hit & ((at & 1) == plane)
                    picked[2 * n + plane][...] = jnp.where(keep, 1.0, 0.0).astype(jnp.bfloat16)

        plain = kl_ref[0].reshape(2 * modes, chans)
        r = lax.broadcasted_iota(jnp.int32, (2 * modes, 2 * modes), 0)
        c = lax.broadcasted_iota(jnp.int32, (2 * modes, 2 * modes), 1)
        odd = (r & 1) == 1
        turn = jnp.where(c == jnp.where(odd, r - 1, r + 1), jnp.where(odd, 1.0, -1.0), 0.0).astype(jnp.bfloat16)
        turned = jnp.dot(turn, plain, preferred_element_type=jnp.float32).astype(jnp.bfloat16)
        for n in range(len(widths)):
            value = jnp.dot(plain, picked[2 * n][...], preferred_element_type=jnp.float32)
            value += jnp.dot(turned, picked[2 * n + 1][...], preferred_element_type=jnp.float32)
            outs[n][0] = value.astype(jnp.bfloat16)

    flops = 4 * rows * 2 * modes * chans * sum(widths)
    nbytes = 2 * (kl_basis.size + rows * 2 * modes * sum(widths))
    return pl.pallas_call(
        kernel,
        grid=(rows,),
        out_shape=[jax.ShapeDtypeStruct((rows, 2 * modes, w), jnp.bfloat16) for w in widths],
        in_specs=[pl.BlockSpec((1, modes, two, chans), lambda i: (i, 0, 0, 0))],
        out_specs=[pl.BlockSpec((1, 2 * modes, w), lambda i: (i, 0, 0)) for w in widths],
        scratch_shapes=[pltpu.VMEM((chans, w), jnp.bfloat16) for w in widths for _ in range(2)],
        compiler_params=pltpu.CompilerParams(vmem_limit_bytes=VMEM_BYTES),
        cost_estimate=pl.CostEstimate(flops=flops, bytes_accessed=nbytes, transcendentals=0),
        name="arrange",
    )(kl_basis)


def project(basis, pieces, total, last):
    rows, out_rows, _ = basis.shape
    svd = pieces[0].shape[2]
    step = math.gcd(rows, 4)
    args = [basis] + list(pieces) + ([] if total is None else [total])

    def kernel(*refs):
        out = refs[-1]
        for m in range(step):
            data = jnp.concatenate([ref[m] for ref in refs[1 : 1 + len(pieces)]], axis=0)
            value = jnp.dot(refs[0][m], data, preferred_element_type=jnp.float32)
            if total is not None:
                value += refs[1 + len(pieces)][m]
            out[m] = value.astype(out.dtype)

    def spec(shape):
        return pl.BlockSpec((step,) + shape, lambda i: (i, 0, 0))

    out_shape = jax.ShapeDtypeStruct((rows, out_rows, svd), jnp.bfloat16 if last else jnp.float32)
    nbytes = sum(a.size * a.dtype.itemsize for a in args) + out_shape.size * out_shape.dtype.itemsize
    return pl.pallas_call(
        kernel,
        grid=(rows // step,),
        out_shape=out_shape,
        in_specs=[spec(a.shape[1:]) for a in args],
        out_specs=spec((out_rows, svd)),
        compiler_params=pltpu.CompilerParams(vmem_limit_bytes=VMEM_BYTES),
        cost_estimate=pl.CostEstimate(flops=2 * basis.size * svd, bytes_accessed=nbytes, transcendentals=0),
        name="project",
    )(*args)


def stages(visibilities, kl_basis, time_flags):
    rows, chans, _, svd = visibilities.shape
    modes = kl_basis.shape[1]
    count = lax.axis_size("ma")
    copies = lax.axis_size("ch")
    total = rows * count
    group = H // rows
    width = chans // group
    unit = width // UNITS
    chunks = [(sum(PARTS[:n]) * unit, part * unit) for n, part in enumerate(PARTS)]
    me = lax.axis_index("ma")
    place = lax.rem(me, group).astype(jnp.int32)

    def swap(x, bits):
        return lax.ppermute(x, "ma", [(i, i ^ bits) for i in range(count)])

    def shift(x, by):
        return lax.ppermute(x, "ma", [(i, (i + by * group) % count) for i in range(count)])

    def sides(x):
        up = shift(x, 1)
        down = shift(x, -1)
        return x, up, down

    (own,) = regroup(visibilities, ((0, 0, width),), width, group)
    firsts = sides(own)
    picks = [(p, offset, size) for offset, size in chunks for p in range(1, group)]
    away = regroup(visibilities, picks, width, group)
    others = []
    for n in range(len(chunks)):
        near = []
        for p in range(1, group):
            near.append(swap(away[n * (group - 1) + p - 1], p))
        near = jnp.stack(near, 0)
        others.append(sides(near))

    mine = lax.dynamic_update_slice(jnp.zeros((total,), jnp.int32), time_flags, (me * rows,))
    flags = mine
    for by in range(1, count // group):
        flags = flags + shift(mine, by)
    bits = group // 2
    while bits:
        flags = flags + swap(flags, bits)
        bits //= 2
    matrix = mixing_matrix(flags, place, rows, group, total)
    bases = arrange_basis(kl_basis, chunks, width, group, copies)

    result = None
    for n, (offset, size) in enumerate(chunks):
        mixed = mix(matrix, firsts, others[n], offset, unit, size)
        back = [mixed[0]]
        for p in range(1, group):
            back.append(swap(mixed[p], p))
        joined = jnp.concatenate([piece.reshape(rows, 2 * size, svd) for piece in back], axis=1)
        pieces = [joined]
        for o in range(1, copies):
            pieces.append(lax.ppermute(joined, "ch", [(i, (i - o) % copies) for i in range(copies)]))
        result = project(bases[n], pieces, result, n == len(chunks) - 1)
    return result.reshape(rows, modes, 2, svd)


def solution(mesh):
    return jax.shard_map(
        stages,
        mesh=mesh,
        in_specs=(P("ma", "ch", None, None), P("ma", "ch", None, None), P("ma")),
        out_specs=P("ma", "ch", None, None),
        check_vma=False,
    )
```

```python
import functools
import math

import jax
import jax.numpy as jnp
from jax import lax
from jax.experimental import pallas as pl
from jax.experimental.pallas import tpu as pltpu
from jax.sharding import PartitionSpec as P


H = 128
UNITS = 8
PARTS = (4, 2, 1, 1)
VMEM_BYTES = 24 << 20


def regroup(visibilities, picks, width, group):
    rows, _, two, svd = visibilities.shape
    shapes = [(size, rows, two, svd) for _, _, size in picks]

    def kernel(src, *refs):
        place = lax.rem(lax.axis_index("ma"), group)
        outs, bufs = refs[: len(picks)], refs[len(picks) : 2 * len(picks)]
        load_sem, store_sem = refs[2 * len(picks) :]
        for n, (partner, offset, size) in enumerate(picks):
            start = lax.bitwise_xor(place, partner) * width + offset

            @pl.loop(0, rows)
            def load(m):
                pltpu.make_async_copy(src.at[m, pl.ds(start, size)], bufs[n].at[:, m], load_sem.at[n]).start()

        stores = []
        for n in range(len(picks)):
            pltpu.make_async_copy(bufs[n], bufs[n], load_sem.at[n]).wait()
            stores.append(pltpu.make_async_copy(bufs[n], outs[n], store_sem.at[n]))
            stores[-1].start()
        for copy in stores:
            copy.wait()

    nbytes = 4 * sum(math.prod(shape) for shape in shapes)
    outs = pl.pallas_call(
        kernel,
        out_shape=[jax.ShapeDtypeStruct(shape, visibilities.dtype) for shape in shapes],
        in_specs=[pl.BlockSpec(memory_space=pltpu.HBM)],
        out_specs=[pl.BlockSpec(memory_space=pl.ANY)] * len(picks),
        scratch_shapes=[pltpu.VMEM(shape, visibilities.dtype) for shape in shapes]
        + [pltpu.SemaphoreType.DMA((len(picks),)), pltpu.SemaphoreType.DMA((len(picks),))],
        cost_estimate=pl.CostEstimate(flops=0, bytes_accessed=nbytes, transcendentals=0),
        name="regroup",
    )(visibilities)
    return [out.reshape(out.shape[0], rows * two, svd) for out in outs]


def mixing_matrix(flags, place, rows, group, total):
    def waves(count):
        at = lax.broadcasted_iota(jnp.int32, (count, total), 0)
        t = lax.broadcasted_iota(jnp.int32, (count, total), 1)
        phases = jnp.mod(row_of(at, place, rows, group) * t + (total // 4) * (at % 2), total)
        phases = phases.astype(jnp.float32) * (2.0 * math.pi / total)
        return jnp.cos(phases), jnp.sin(phases)

    outs, ins = 2 * rows * group, 6 * rows * group
    co, so, ci, si = lax.optimization_barrier(waves(outs) + waves(ins))
    kept = flags.astype(jnp.float32)
    dot = functools.partial(
        lax.dot_general, dimension_numbers=(((1,), (1,)), ((), ())), precision=lax.Precision.HIGHEST
    )
    taps = (dot(co * kept, ci) + dot(so * kept, si)) / total
    out_row = row_of(lax.broadcasted_iota(jnp.int32, taps.shape, 0), place, rows, group)
    in_row = row_of(lax.broadcasted_iota(jnp.int32, taps.shape, 1), place, rows, group)
    return jnp.where(jnp.abs(out_row - in_row) <= H, taps, 0.0).astype(jnp.bfloat16)


def row_of(at, place, rows, group):
    row = (at // 2) % rows
    block = lax.bitwise_xor((at // (2 * rows)) % group, place)
    side = at // (2 * rows * group)
    return block * rows + row + jnp.where(side == 1, -H, jnp.where(side == 2, H, 0))


def mix(matrix, firsts, others, offset, unit, size):
    pair_rows, svd = firsts[0].shape[1:]
    group = matrix.shape[0] // pair_rows
    rows = pair_rows // 2
    start = offset // unit

    def kernel(t_ref, *refs):
        ins, outs = refs[:6], refs[6:]
        table = t_ref[...]
        for c in range(0, unit, 2):
            stack = []
            for first, other in zip(ins[:3], ins[3:]):
                stack.append(jnp.concatenate([first[c], first[c + 1]], axis=1))
                for p in range(group - 1):
                    stack.append(jnp.concatenate([other[p, c], other[p, c + 1]], axis=1))
            data = jnp.concatenate(stack, axis=0)
            mixed = jnp.dot(table, data, preferred_element_type=jnp.float32).astype(jnp.bfloat16)
            for r in range(group):
                part = mixed[r * pair_rows : (r + 1) * pair_rows]
                outs[r][:, c] = part[:, :svd].reshape(rows, 2, svd)
                outs[r][:, c + 1] = part[:, svd:].reshape(rows, 2, svd)

    flops = 2 * matrix.size * size * svd
    nbytes = 2 * (matrix.size + 4 * group * size * pair_rows * svd)
    return pl.pallas_call(
        kernel,
        grid=(size // unit,),
        out_shape=[jax.ShapeDtypeStruct((rows, size, 2, svd), jnp.bfloat16)] * group,
        in_specs=[pl.BlockSpec(matrix.shape, lambda i: (0, 0))]
        + [pl.BlockSpec((unit, pair_rows, svd), lambda i: (start + i, 0, 0))] * 3
        + [pl.BlockSpec((group - 1, unit, pair_rows, svd), lambda i: (0, i, 0, 0))] * 3,
        out_specs=[pl.BlockSpec((rows, unit, 2, svd), lambda i: (0, i, 0, 0))] * group,
        compiler_params=pltpu.CompilerParams(vmem_limit_bytes=VMEM_BYTES),
        cost_estimate=pl.CostEstimate(flops=flops, bytes_accessed=nbytes, transcendentals=0),
        name="mix",
    )(matrix, *firsts, *others)


def mix_apart(matrix, first, others):
    size, pair_rows, svd = first.shape
    depth = matrix.shape[0]
    group = depth // pair_rows
    rows = pair_rows // 2
    sides = matrix.shape[1] // depth

    def kernel(t_ref, f_ref, o_ref, *outs):
        for c in range(0, size, 2):
            stack = [jnp.concatenate([f_ref[c], f_ref[c + 1]], axis=1)]
            for p in range(group - 1):
                stack.append(jnp.concatenate([o_ref[p, c], o_ref[p, c + 1]], axis=1))
            data = jnp.concatenate(stack, axis=0)
            for side in range(sides):
                table = t_ref[:, side * depth : (side + 1) * depth]
                mixed = jnp.dot(table, data, preferred_element_type=jnp.float32).astype(jnp.bfloat16)
                for r in range(group):
                    part = mixed[r * pair_rows : (r + 1) * pair_rows]
                    outs[r][side, :, c] = part[:, :svd].reshape(rows, 2, svd)
                    outs[r][side, :, c + 1] = part[:, svd:].reshape(rows, 2, svd)

    flops = 2 * matrix.size * size * svd
    nbytes = 2 * (matrix.size + (1 + sides) * group * size * pair_rows * svd)
    return pl.pallas_call(
        kernel,
        out_shape=[jax.ShapeDtypeStruct((sides, rows, size, 2, svd), jnp.bfloat16)] * group,
        compiler_params=pltpu.CompilerParams(vmem_limit_bytes=VMEM_BYTES),
        cost_estimate=pl.CostEstimate(flops=flops, bytes_accessed=nbytes, transcendentals=0),
        name="mix_apart",
    )(matrix, first, others)


def arrange_basis(kl_basis, chunks, width, group, copies):
    rows, modes, two, chans = kl_basis.shape
    pieces = copies * group
    widths = [2 * pieces * size for _, size in chunks]

    def kernel(kl_ref, *refs):
        outs, picked = refs[: len(chunks)], refs[len(chunks) :]

        @pl.when(pl.program_id(0) == 0)
        def _():
            place = lax.rem(lax.axis_index("ma"), group)
            core = lax.axis_index("ch")
            for n, (offset, size) in enumerate(chunks):
                at = lax.broadcasted_iota(jnp.int32, (1, widths[n]), 1)
                begin = jnp.zeros_like(at)
                for piece in range(pieces):
                    source = lax.rem(core + piece // group, copies)
                    quarter = lax.bitwise_xor(place, piece % group)
                    first = source * group * width + quarter * width + offset - piece * size
                    begin = jnp.where(at >= 2 * piece * size, first, begin)
                hit = begin + (at >> 1) == lax.broadcasted_iota(jnp.int32, (chans, widths[n]), 0)
                for plane in range(2):
                    keep = hit & ((at & 1) == plane)
                    picked[2 * n + plane][...] = jnp.where(keep, 1.0, 0.0).astype(jnp.bfloat16)

        plain = kl_ref[0].reshape(2 * modes, chans)
        r = lax.broadcasted_iota(jnp.int32, (2 * modes, 2 * modes), 0)
        c = lax.broadcasted_iota(jnp.int32, (2 * modes, 2 * modes), 1)
        odd = (r & 1) == 1
        turn = jnp.where(c == jnp.where(odd, r - 1, r + 1), jnp.where(odd, 1.0, -1.0), 0.0).astype(jnp.bfloat16)
        turned = jnp.dot(turn, plain, preferred_element_type=jnp.float32).astype(jnp.bfloat16)
        for n in range(len(widths)):
            value = jnp.dot(plain, picked[2 * n][...], preferred_element_type=jnp.float32)
            value += jnp.dot(turned, picked[2 * n + 1][...], preferred_element_type=jnp.float32)
            outs[n][0] = value.astype(jnp.bfloat16)

    flops = 4 * rows * 2 * modes * chans * sum(widths)
    nbytes = 2 * (kl_basis.size + rows * 2 * modes * sum(widths))
    return pl.pallas_call(
        kernel,
        grid=(rows,),
        out_shape=[jax.ShapeDtypeStruct((rows, 2 * modes, w), jnp.bfloat16) for w in widths],
        in_specs=[pl.BlockSpec((1, modes, two, chans), lambda i: (i, 0, 0, 0))],
        out_specs=[pl.BlockSpec((1, 2 * modes, w), lambda i: (i, 0, 0)) for w in widths],
        scratch_shapes=[pltpu.VMEM((chans, w), jnp.bfloat16) for w in widths for _ in range(2)],
        compiler_params=pltpu.CompilerParams(vmem_limit_bytes=VMEM_BYTES),
        cost_estimate=pl.CostEstimate(flops=flops, bytes_accessed=nbytes, transcendentals=0),
        name="arrange",
    )(kl_basis)


def project(basis, pieces, total, last):
    rows, out_rows, _ = basis.shape
    svd = pieces[0].shape[2]
    step = math.gcd(rows, 4)
    args = [basis] + list(pieces) + ([] if total is None else [total])

    def kernel(*refs):
        out = refs[-1]
        for m in range(step):
            data = jnp.concatenate([ref[m] for ref in refs[1 : 1 + len(pieces)]], axis=0)
            value = jnp.dot(refs[0][m], data, preferred_element_type=jnp.float32)
            if total is not None:
                value += refs[1 + len(pieces)][m]
            out[m] = value.astype(out.dtype)

    def spec(shape):
        return pl.BlockSpec((step,) + shape, lambda i: (i, 0, 0))

    out_shape = jax.ShapeDtypeStruct((rows, out_rows, svd), jnp.bfloat16 if last else jnp.float32)
    nbytes = sum(a.size * a.dtype.itemsize for a in args) + out_shape.size * out_shape.dtype.itemsize
    return pl.pallas_call(
        kernel,
        grid=(rows // step,),
        out_shape=out_shape,
        in_specs=[spec(a.shape[1:]) for a in args],
        out_specs=spec((out_rows, svd)),
        compiler_params=pltpu.CompilerParams(vmem_limit_bytes=VMEM_BYTES),
        cost_estimate=pl.CostEstimate(flops=2 * basis.size * svd, bytes_accessed=nbytes, transcendentals=0),
        name="project",
    )(*args)


def stages(visibilities, kl_basis, time_flags):
    rows, chans, _, svd = visibilities.shape
    modes = kl_basis.shape[1]
    count = lax.axis_size("ma")
    copies = lax.axis_size("ch")
    total = rows * count
    group = H // rows
    width = chans // group
    unit = width // UNITS
    chunks = [(sum(PARTS[:n]) * unit, part * unit) for n, part in enumerate(PARTS)]
    me = lax.axis_index("ma")
    place = lax.rem(me, group).astype(jnp.int32)

    def swap(x, bits):
        return lax.ppermute(x, "ma", [(i, i ^ bits) for i in range(count)])

    def shift(x, by):
        return lax.ppermute(x, "ma", [(i, (i + by * group) % count) for i in range(count)])

    def sides(x):
        up = shift(x, 1)
        down = shift(x, -1)
        return x, up, down

    last = len(chunks) - 1
    begin, tail = chunks[last]
    (own,) = regroup(visibilities, ((0, 0, begin),), width, group)
    firsts = sides(own)
    picks = [(p, offset, size) for offset, size in chunks for p in range(1, group)] + [(0, begin, tail)]
    away = regroup(visibilities, picks, width, group)
    others = []
    for n in range(len(chunks)):
        near = []
        for p in range(1, group):
            near.append(swap(away[n * (group - 1) + p - 1], p))
        near = jnp.stack(near, 0)
        others.append(sides(near) if n < last else near)

    mine = lax.dynamic_update_slice(jnp.zeros((total,), jnp.int32), time_flags, (me * rows,))
    flags = mine
    for by in range(1, count // group):
        flags = flags + shift(mine, by)
    bits = group // 2
    while bits:
        flags = flags + swap(flags, bits)
        bits //= 2
    matrix = mixing_matrix(flags, place, rows, group, total)
    bases = arrange_basis(kl_basis, chunks, width, group, copies)

    def returned(pieces):
        back = [pieces[0]]
        for p in range(1, group):
            back.append(swap(pieces[p], p))
        return [piece.reshape(piece.shape[:-3] + (2 * piece.shape[-3], svd)) for piece in back]

    shares = mix_apart(matrix, away[-1], others[last])
    shares = returned(shares)
    kept, rise, fall = [jnp.concatenate([share[side] for share in shares], axis=1) for side in range(3)]
    rise = shift(rise, 1)
    fall = shift(fall, -1)

    result = None
    for n, (offset, size) in enumerate(chunks):
        if n < last:
            mixed = mix(matrix, firsts, others[n], offset, unit, size)
            back = returned(mixed)
            joined = jnp.concatenate(back, axis=1)
        else:
            wide = [share.astype(jnp.float32) for share in (kept, rise, fall)]
            joined = (wide[0] + wide[1] + wide[2]).astype(jnp.bfloat16)
        pieces = [joined]
        for o in range(1, copies):
            pieces.append(lax.ppermute(joined, "ch", [(i, (i - o) % copies) for i in range(copies)]))
        result = project(bases[n], pieces, result, n == last)
    return result.reshape(rows, modes, 2, svd)


def solution(mesh):
    return jax.shard_map(
        stages,
        mesh=mesh,
        in_specs=(P("ma", "ch", None, None), P("ma", "ch", None, None), P("ma")),
        out_specs=P("ma", "ch", None, None),
        check_vma=False,
    )
```

```python
import functools
import math

import jax
import jax.numpy as jnp
from jax import lax
from jax.experimental import pallas as pl
from jax.experimental.pallas import tpu as pltpu
from jax.sharding import PartitionSpec as P


H = 128
UNITS = 8
PARTS = (4, 2, 1, 1)
VMEM_BYTES = 24 << 20


def regroup(visibilities, picks, width, group):
    rows, _, two, svd = visibilities.shape
    shapes = [(size, rows, two, svd) for _, _, size in picks]

    def kernel(src, *refs):
        place = lax.rem(lax.axis_index("ma"), group)
        outs, bufs = refs[: len(picks)], refs[len(picks) : 2 * len(picks)]
        load_sem, store_sem = refs[2 * len(picks) :]
        for n, (partner, offset, size) in enumerate(picks):
            start = lax.bitwise_xor(place, partner) * width + offset

            @pl.loop(0, rows)
            def load(m):
                pltpu.make_async_copy(src.at[m, pl.ds(start, size)], bufs[n].at[:, m], load_sem.at[n]).start()

        stores = []
        for n in range(len(picks)):
            pltpu.make_async_copy(bufs[n], bufs[n], load_sem.at[n]).wait()
            stores.append(pltpu.make_async_copy(bufs[n], outs[n], store_sem.at[n]))
            stores[-1].start()
        for copy in stores:
            copy.wait()

    nbytes = 4 * sum(math.prod(shape) for shape in shapes)
    outs = pl.pallas_call(
        kernel,
        out_shape=[jax.ShapeDtypeStruct(shape, visibilities.dtype) for shape in shapes],
        in_specs=[pl.BlockSpec(memory_space=pltpu.HBM)],
        out_specs=[pl.BlockSpec(memory_space=pl.ANY)] * len(picks),
        scratch_shapes=[pltpu.VMEM(shape, visibilities.dtype) for shape in shapes]
        + [pltpu.SemaphoreType.DMA((len(picks),)), pltpu.SemaphoreType.DMA((len(picks),))],
        cost_estimate=pl.CostEstimate(flops=0, bytes_accessed=nbytes, transcendentals=0),
        name="regroup",
    )(visibilities)
    return [out.reshape(out.shape[0], rows * two, svd) for out in outs]


def regroup_own(visibilities, width, size, group):
    rows, _, two, svd = visibilities.shape
    shape = (size, rows, two, svd)

    def kernel(src, out, sem):
        start = lax.rem(lax.axis_index("ma"), group) * width

        @pl.loop(0, rows)
        def load(m):
            pltpu.make_async_copy(src.at[m, pl.ds(start, size)], out.at[:, m], sem).start()

        pltpu.make_async_copy(out, out, sem).wait()

    out = pl.pallas_call(
        kernel,
        out_shape=jax.ShapeDtypeStruct(shape, visibilities.dtype),
        in_specs=[pl.BlockSpec(memory_space=pltpu.HBM)],
        scratch_shapes=[pltpu.SemaphoreType.DMA],
        cost_estimate=pl.CostEstimate(flops=0, bytes_accessed=4 * math.prod(shape), transcendentals=0),
        name="regroup_own",
    )(visibilities)
    return out.reshape(size, rows * two, svd)


def mixing_matrix(flags, place, rows, group, total):
    def waves(count):
        at = lax.broadcasted_iota(jnp.int32, (count, total), 0)
        t = lax.broadcasted_iota(jnp.int32, (count, total), 1)
        phases = jnp.mod(row_of(at, place, rows, group) * t + (total // 4) * (at % 2), total)
        phases = phases.astype(jnp.float32) * (2.0 * math.pi / total)
        return jnp.cos(phases), jnp.sin(phases)

    outs, ins = 2 * rows * group, 6 * rows * group
    co, so, ci, si = lax.optimization_barrier(waves(outs) + waves(ins))
    kept = flags.astype(jnp.float32)
    dot = functools.partial(
        lax.dot_general, dimension_numbers=(((1,), (1,)), ((), ())), precision=lax.Precision.HIGHEST
    )
    taps = (dot(co * kept, ci) + dot(so * kept, si)) / total
    out_row = row_of(lax.broadcasted_iota(jnp.int32, taps.shape, 0), place, rows, group)
    in_row = row_of(lax.broadcasted_iota(jnp.int32, taps.shape, 1), place, rows, group)
    return jnp.where(jnp.abs(out_row - in_row) <= H, taps, 0.0).astype(jnp.bfloat16)


def row_of(at, place, rows, group):
    row = (at // 2) % rows
    block = lax.bitwise_xor((at // (2 * rows)) % group, place)
    side = at // (2 * rows * group)
    return block * rows + row + jnp.where(side == 1, -H, jnp.where(side == 2, H, 0))


def mix(matrix, firsts, others, offset, unit, size):
    pair_rows, svd = firsts[0].shape[1:]
    group = matrix.shape[0] // pair_rows
    rows = pair_rows // 2
    start = offset // unit

    def kernel(t_ref, *refs):
        ins, outs = refs[:6], refs[6:]
        table = t_ref[...]
        for c in range(0, unit, 2):
            stack = []
            for first, other in zip(ins[:3], ins[3:]):
                stack.append(jnp.concatenate([first[c], first[c + 1]], axis=1))
                for p in range(group - 1):
                    stack.append(jnp.concatenate([other[p, c], other[p, c + 1]], axis=1))
            data = jnp.concatenate(stack, axis=0)
            mixed = jnp.dot(table, data, preferred_element_type=jnp.float32).astype(jnp.bfloat16)
            for r in range(group):
                part = mixed[r * pair_rows : (r + 1) * pair_rows]
                outs[r][:, c] = part[:, :svd].reshape(rows, 2, svd)
                outs[r][:, c + 1] = part[:, svd:].reshape(rows, 2, svd)

    flops = 2 * matrix.size * size * svd
    nbytes = 2 * (matrix.size + 4 * group * size * pair_rows * svd)
    return pl.pallas_call(
        kernel,
        grid=(size // unit,),
        out_shape=[jax.ShapeDtypeStruct((rows, size, 2, svd), jnp.bfloat16)] * group,
        in_specs=[pl.BlockSpec(matrix.shape, lambda i: (0, 0))]
        + [pl.BlockSpec((unit, pair_rows, svd), lambda i: (start + i, 0, 0))] * 3
        + [pl.BlockSpec((group - 1, unit, pair_rows, svd), lambda i: (0, i, 0, 0))] * 3,
        out_specs=[pl.BlockSpec((rows, unit, 2, svd), lambda i: (0, i, 0, 0))] * group,
        compiler_params=pltpu.CompilerParams(vmem_limit_bytes=VMEM_BYTES),
        cost_estimate=pl.CostEstimate(flops=flops, bytes_accessed=nbytes, transcendentals=0),
        name="mix",
    )(matrix, *firsts, *others)


def mix_apart(matrix, first, others):
    size, pair_rows, svd = first.shape
    depth = matrix.shape[0]
    group = depth // pair_rows
    rows = pair_rows // 2
    sides = matrix.shape[1] // depth

    def kernel(t_ref, f_ref, o_ref, *outs):
        for c in range(0, size, 2):
            stack = [jnp.concatenate([f_ref[c], f_ref[c + 1]], axis=1)]
            for p in range(group - 1):
                stack.append(jnp.concatenate([o_ref[p, c], o_ref[p, c + 1]], axis=1))
            data = jnp.concatenate(stack, axis=0)
            for side in range(sides):
                table = t_ref[:, side * depth : (side + 1) * depth]
                mixed = jnp.dot(table, data, preferred_element_type=jnp.float32).astype(jnp.bfloat16)
                for r in range(group):
                    part = mixed[r * pair_rows : (r + 1) * pair_rows]
                    outs[r][side, :, c] = part[:, :svd].reshape(rows, 2, svd)
                    outs[r][side, :, c + 1] = part[:, svd:].reshape(rows, 2, svd)

    flops = 2 * matrix.size * size * svd
    nbytes = 2 * (matrix.size + (1 + sides) * group * size * pair_rows * svd)
    return pl.pallas_call(
        kernel,
        out_shape=[jax.ShapeDtypeStruct((sides, rows, size, 2, svd), jnp.bfloat16)] * group,
        compiler_params=pltpu.CompilerParams(vmem_limit_bytes=VMEM_BYTES),
        cost_estimate=pl.CostEstimate(flops=flops, bytes_accessed=nbytes, transcendentals=0),
        name="mix_apart",
    )(matrix, first, others)


def arrange_basis(kl_basis, chunks, width, group, copies):
    rows, modes, two, chans = kl_basis.shape
    pieces = copies * group
    widths = [2 * pieces * size for _, size in chunks]

    def kernel(kl_ref, *refs):
        outs, picked = refs[: len(chunks)], refs[len(chunks) :]

        @pl.when(pl.program_id(0) == 0)
        def _():
            place = lax.rem(lax.axis_index("ma"), group)
            core = lax.axis_index("ch")
            for n, (offset, size) in enumerate(chunks):
                at = lax.broadcasted_iota(jnp.int32, (1, widths[n]), 1)
                begin = jnp.zeros_like(at)
                for piece in range(pieces):
                    source = lax.rem(core + piece // group, copies)
                    quarter = lax.bitwise_xor(place, piece % group)
                    first = source * group * width + quarter * width + offset - piece * size
                    begin = jnp.where(at >= 2 * piece * size, first, begin)
                hit = begin + (at >> 1) == lax.broadcasted_iota(jnp.int32, (chans, widths[n]), 0)
                for plane in range(2):
                    keep = hit & ((at & 1) == plane)
                    picked[2 * n + plane][...] = jnp.where(keep, 1.0, 0.0).astype(jnp.bfloat16)

        plain = kl_ref[0].reshape(2 * modes, chans)
        r = lax.broadcasted_iota(jnp.int32, (2 * modes, 2 * modes), 0)
        c = lax.broadcasted_iota(jnp.int32, (2 * modes, 2 * modes), 1)
        odd = (r & 1) == 1
        turn = jnp.where(c == jnp.where(odd, r - 1, r + 1), jnp.where(odd, 1.0, -1.0), 0.0).astype(jnp.bfloat16)
        turned = jnp.dot(turn, plain, preferred_element_type=jnp.float32).astype(jnp.bfloat16)
        for n in range(len(widths)):
            value = jnp.dot(plain, picked[2 * n][...], preferred_element_type=jnp.float32)
            value += jnp.dot(turned, picked[2 * n + 1][...], preferred_element_type=jnp.float32)
            outs[n][0] = value.astype(jnp.bfloat16)

    flops = 4 * rows * 2 * modes * chans * sum(widths)
    nbytes = 2 * (kl_basis.size + rows * 2 * modes * sum(widths))
    return pl.pallas_call(
        kernel,
        grid=(rows,),
        out_shape=[jax.ShapeDtypeStruct((rows, 2 * modes, w), jnp.bfloat16) for w in widths],
        in_specs=[pl.BlockSpec((1, modes, two, chans), lambda i: (i, 0, 0, 0))],
        out_specs=[pl.BlockSpec((1, 2 * modes, w), lambda i: (i, 0, 0)) for w in widths],
        scratch_shapes=[pltpu.VMEM((chans, w), jnp.bfloat16) for w in widths for _ in range(2)],
        compiler_params=pltpu.CompilerParams(vmem_limit_bytes=VMEM_BYTES),
        cost_estimate=pl.CostEstimate(flops=flops, bytes_accessed=nbytes, transcendentals=0),
        name="arrange",
    )(kl_basis)


def project(basis, pieces, total):
    rows, out_rows, _ = basis.shape
    svd = pieces[0].shape[2]
    step = math.gcd(rows, 4)
    args = [basis] + list(pieces) + ([] if total is None else [total])

    def kernel(*refs):
        out = refs[-1]
        for m in range(step):
            data = jnp.concatenate([ref[m] for ref in refs[1 : 1 + len(pieces)]], axis=0)
            value = jnp.dot(refs[0][m], data, preferred_element_type=jnp.float32)
            if total is not None:
                value += refs[1 + len(pieces)][m]
            out[m] = value.astype(out.dtype)

    def spec(shape):
        return pl.BlockSpec((step,) + shape, lambda i: (i, 0, 0))

    out_shape = jax.ShapeDtypeStruct((rows, out_rows, svd), jnp.float32)
    nbytes = sum(a.size * a.dtype.itemsize for a in args) + out_shape.size * out_shape.dtype.itemsize
    return pl.pallas_call(
        kernel,
        grid=(rows // step,),
        out_shape=out_shape,
        in_specs=[spec(a.shape[1:]) for a in args],
        out_specs=spec((out_rows, svd)),
        compiler_params=pltpu.CompilerParams(vmem_limit_bytes=VMEM_BYTES),
        cost_estimate=pl.CostEstimate(flops=2 * basis.size * svd, bytes_accessed=nbytes, transcendentals=0),
        name="project",
    )(*args)


def project_last(basis, pieces, total):
    rows, out_rows, width = basis.shape
    svd = pieces[0].shape[2]
    block = math.gcd(rows, 4)

    def kernel(a_ref, *refs):
        data_refs, t_ref, out, buf, sem = refs[: len(pieces)], *refs[len(pieces) :]
        empty = jnp.zeros((width, svd), jnp.bfloat16)

        @pl.loop(0, rows // block)
        def step(n):
            for m in range(0, block, 2):
                at = n * block + m
                left = jnp.concatenate([a_ref[at], a_ref[at + 1]], axis=1)
                one = jnp.concatenate([ref[at] for ref in data_refs], axis=0)
                two = jnp.concatenate([ref[at + 1] for ref in data_refs], axis=0)
                right = jnp.concatenate(
                    [jnp.concatenate([one, empty], axis=1), jnp.concatenate([empty, two], axis=1)], axis=0
                )
                value = jnp.dot(left, right, preferred_element_type=jnp.float32)
                buf[at] = (value[:, :svd] + t_ref[at]).astype(buf.dtype)
                buf[at + 1] = (value[:, svd:] + t_ref[at + 1]).astype(buf.dtype)
            span = pl.ds(n * block, block)
            pltpu.make_async_copy(buf.at[span], out.at[span], sem).start()

        pltpu.make_async_copy(buf, out, sem).wait()

    args = [basis, *pieces, total]
    out_shape = jax.ShapeDtypeStruct((rows, out_rows, svd), jnp.bfloat16)
    nbytes = sum(a.size * a.dtype.itemsize for a in args) + out_shape.size * 2
    return pl.pallas_call(
        kernel,
        out_shape=out_shape,
        out_specs=pl.BlockSpec(memory_space=pl.ANY),
        scratch_shapes=[pltpu.VMEM(out_shape.shape, out_shape.dtype), pltpu.SemaphoreType.DMA],
        compiler_params=pltpu.CompilerParams(vmem_limit_bytes=VMEM_BYTES),
        cost_estimate=pl.CostEstimate(flops=2 * basis.size * svd, bytes_accessed=nbytes, transcendentals=0),
        name="project_last",
    )(*args)


def stages(visibilities, kl_basis, time_flags):
    rows, chans, _, svd = visibilities.shape
    modes = kl_basis.shape[1]
    count = lax.axis_size("ma")
    copies = lax.axis_size("ch")
    total = rows * count
    group = H // rows
    width = chans // group
    unit = width // UNITS
    chunks = [(sum(PARTS[:n]) * unit, part * unit) for n, part in enumerate(PARTS)]
    me = lax.axis_index("ma")
    place = lax.rem(me, group).astype(jnp.int32)

    def swap(x, bits):
        return lax.ppermute(x, "ma", [(i, i ^ bits) for i in range(count)])

    def shift(x, by):
        return lax.ppermute(x, "ma", [(i, (i + by * group) % count) for i in range(count)])

    def sides(x):
        up = shift(x, 1)
        down = shift(x, -1)
        return x, up, down

    last = len(chunks) - 1
    begin, tail = chunks[last]
    own = regroup_own(visibilities, width, begin, group)
    firsts = sides(own)
    picks = [(p, offset, size) for offset, size in chunks for p in range(1, group)] + [(0, begin, tail)]
    away = regroup(visibilities, picks, width, group)
    others = []
    for n in range(len(chunks)):
        near = []
        for p in range(1, group):
            near.append(swap(away[n * (group - 1) + p - 1], p))
        near = jnp.stack(near, 0)
        others.append(sides(near) if n < last else near)

    mine = lax.dynamic_update_slice(jnp.zeros((total,), jnp.int32), time_flags, (me * rows,))
    flags = mine
    for by in range(1, count // group):
        flags = flags + shift(mine, by)
    bits = group // 2
    while bits:
        flags = flags + swap(flags, bits)
        bits //= 2
    matrix = mixing_matrix(flags, place, rows, group, total)
    bases = arrange_basis(kl_basis, chunks, width, group, copies)

    def returned(pieces):
        back = [pieces[0]]
        for p in range(1, group):
            back.append(swap(pieces[p], p))
        return [piece.reshape(piece.shape[:-3] + (2 * piece.shape[-3], svd)) for piece in back]

    shares = mix_apart(matrix, away[-1], others[last])
    shares = returned(shares)
    kept, rise, fall = [jnp.concatenate([share[side] for share in shares], axis=1) for side in range(3)]
    rise = shift(rise, 1)
    fall = shift(fall, -1)

    result = None
    for n, (offset, size) in enumerate(chunks):
        if n < last:
            mixed = mix(matrix, firsts, others[n], offset, unit, size)
            back = returned(mixed)
            joined = jnp.concatenate(back, axis=1)
        else:
            wide = [share.astype(jnp.float32) for share in (kept, rise, fall)]
            joined = (wide[0] + wide[1] + wide[2]).astype(jnp.bfloat16)
        pieces = [joined]
        for o in range(1, copies):
            pieces.append(lax.ppermute(joined, "ch", [(i, (i - o) % copies) for i in range(copies)]))
        result = (project_last if n == last else project)(bases[n], pieces, result)
    return result.reshape(rows, modes, 2, svd)


def solution(mesh):
    return jax.shard_map(
        stages,
        mesh=mesh,
        in_specs=(P("ma", "ch", None, None), P("ma", "ch", None, None), P("ma")),
        out_specs=P("ma", "ch", None, None),
        check_vma=False,
    )
```

```python
import functools
import math

import jax
import jax.numpy as jnp
from jax import lax
from jax.experimental import pallas as pl
from jax.experimental.pallas import tpu as pltpu
from jax.sharding import PartitionSpec as P


H = 128
UNITS = 8
PARTS = (5, 2, 1)
VMEM_BYTES = 24 << 20


def regroup(visibilities, picks, width, group):
    rows, _, two, svd = visibilities.shape
    shapes = [(size, rows, two, svd) for _, _, size in picks]

    def kernel(src, *refs):
        place = lax.rem(lax.axis_index("ma"), group)
        outs, bufs = refs[: len(picks)], refs[len(picks) : 2 * len(picks)]
        load_sem, store_sem = refs[2 * len(picks) :]
        for n, (partner, offset, size) in enumerate(picks):
            start = lax.bitwise_xor(place, partner) * width + offset

            @pl.loop(0, rows)
            def load(m):
                pltpu.make_async_copy(src.at[m, pl.ds(start, size)], bufs[n].at[:, m], load_sem.at[n]).start()

        stores = []
        for n in range(len(picks)):
            pltpu.make_async_copy(bufs[n], bufs[n], load_sem.at[n]).wait()
            stores.append(pltpu.make_async_copy(bufs[n], outs[n], store_sem.at[n]))
            stores[-1].start()
        for copy in stores:
            copy.wait()

    nbytes = 4 * sum(math.prod(shape) for shape in shapes)
    outs = pl.pallas_call(
        kernel,
        out_shape=[jax.ShapeDtypeStruct(shape, visibilities.dtype) for shape in shapes],
        in_specs=[pl.BlockSpec(memory_space=pltpu.HBM)],
        out_specs=[pl.BlockSpec(memory_space=pl.ANY)] * len(picks),
        scratch_shapes=[pltpu.VMEM(shape, visibilities.dtype) for shape in shapes]
        + [pltpu.SemaphoreType.DMA((len(picks),)), pltpu.SemaphoreType.DMA((len(picks),))],
        cost_estimate=pl.CostEstimate(flops=0, bytes_accessed=nbytes, transcendentals=0),
        name="regroup",
    )(visibilities)
    return [out.reshape(out.shape[0], rows * two, svd) for out in outs]


def regroup_own(visibilities, width, size, group):
    rows, _, two, svd = visibilities.shape
    shape = (size, rows, two, svd)

    def kernel(src, out, sem):
        start = lax.rem(lax.axis_index("ma"), group) * width

        @pl.loop(0, rows)
        def load(m):
            pltpu.make_async_copy(src.at[m, pl.ds(start, size)], out.at[:, m], sem).start()

        pltpu.make_async_copy(out, out, sem).wait()

    out = pl.pallas_call(
        kernel,
        out_shape=jax.ShapeDtypeStruct(shape, visibilities.dtype),
        in_specs=[pl.BlockSpec(memory_space=pltpu.HBM)],
        scratch_shapes=[pltpu.SemaphoreType.DMA],
        cost_estimate=pl.CostEstimate(flops=0, bytes_accessed=4 * math.prod(shape), transcendentals=0),
        name="regroup_own",
    )(visibilities)
    return out.reshape(size, rows * two, svd)


def mixing_matrix(flags, place, rows, group, total):
    def waves(count):
        at = lax.broadcasted_iota(jnp.int32, (count, total), 0)
        t = lax.broadcasted_iota(jnp.int32, (count, total), 1)
        phases = jnp.mod(row_of(at, place, rows, group) * t + (total // 4) * (at % 2), total)
        phases = phases.astype(jnp.float32) * (2.0 * math.pi / total)
        return jnp.cos(phases), jnp.sin(phases)

    outs, ins = 2 * rows * group, 6 * rows * group
    co, so, ci, si = lax.optimization_barrier(waves(outs) + waves(ins))
    kept = flags.astype(jnp.float32)
    dot = functools.partial(
        lax.dot_general, dimension_numbers=(((1,), (1,)), ((), ())), precision=lax.Precision.HIGHEST
    )
    taps = (dot(co * kept, ci) + dot(so * kept, si)) / total
    out_row = row_of(lax.broadcasted_iota(jnp.int32, taps.shape, 0), place, rows, group)
    in_row = row_of(lax.broadcasted_iota(jnp.int32, taps.shape, 1), place, rows, group)
    return jnp.where(jnp.abs(out_row - in_row) <= H, taps, 0.0).astype(jnp.bfloat16)


def row_of(at, place, rows, group):
    row = (at // 2) % rows
    block = lax.bitwise_xor((at // (2 * rows)) % group, place)
    side = at // (2 * rows * group)
    return block * rows + row + jnp.where(side == 1, -H, jnp.where(side == 2, H, 0))


def mix(matrix, firsts, others, offset, unit, size):
    pair_rows, svd = firsts[0].shape[1:]
    group = matrix.shape[0] // pair_rows
    rows = pair_rows // 2
    start = offset // unit

    def kernel(t_ref, *refs):
        ins, outs = refs[:6], refs[6:]
        table = t_ref[...]
        for c in range(0, unit, 2):
            stack = []
            for first, other in zip(ins[:3], ins[3:]):
                stack.append(jnp.concatenate([first[c], first[c + 1]], axis=1))
                for p in range(group - 1):
                    stack.append(jnp.concatenate([other[p, c], other[p, c + 1]], axis=1))
            data = jnp.concatenate(stack, axis=0)
            mixed = jnp.dot(table, data, preferred_element_type=jnp.float32).astype(jnp.bfloat16)
            for r in range(group):
                part = mixed[r * pair_rows : (r + 1) * pair_rows]
                outs[r][:, c] = part[:, :svd].reshape(rows, 2, svd)
                outs[r][:, c + 1] = part[:, svd:].reshape(rows, 2, svd)

    flops = 2 * matrix.size * size * svd
    nbytes = 2 * (matrix.size + 4 * group * size * pair_rows * svd)
    return pl.pallas_call(
        kernel,
        grid=(size // unit,),
        out_shape=[jax.ShapeDtypeStruct((rows, size, 2, svd), jnp.bfloat16)] * group,
        in_specs=[pl.BlockSpec(matrix.shape, lambda i: (0, 0))]
        + [pl.BlockSpec((unit, pair_rows, svd), lambda i: (start + i, 0, 0))] * 3
        + [pl.BlockSpec((group - 1, unit, pair_rows, svd), lambda i: (0, i, 0, 0))] * 3,
        out_specs=[pl.BlockSpec((rows, unit, 2, svd), lambda i: (0, i, 0, 0))] * group,
        compiler_params=pltpu.CompilerParams(vmem_limit_bytes=VMEM_BYTES),
        cost_estimate=pl.CostEstimate(flops=flops, bytes_accessed=nbytes, transcendentals=0),
        name="mix",
    )(matrix, *firsts, *others)


def mix_apart(matrix, first, others):
    size, pair_rows, svd = first.shape
    depth = matrix.shape[0]
    group = depth // pair_rows
    rows = pair_rows // 2
    sides = matrix.shape[1] // depth

    def kernel(t_ref, f_ref, o_ref, *outs):
        for c in range(0, size, 2):
            stack = [jnp.concatenate([f_ref[c], f_ref[c + 1]], axis=1)]
            for p in range(group - 1):
                stack.append(jnp.concatenate([o_ref[p, c], o_ref[p, c + 1]], axis=1))
            data = jnp.concatenate(stack, axis=0)
            for side in range(sides):
                table = t_ref[:, side * depth : (side + 1) * depth]
                mixed = jnp.dot(table, data, preferred_element_type=jnp.float32).astype(jnp.bfloat16)
                for r in range(group):
                    part = mixed[r * pair_rows : (r + 1) * pair_rows]
                    outs[r][side, :, c] = part[:, :svd].reshape(rows, 2, svd)
                    outs[r][side, :, c + 1] = part[:, svd:].reshape(rows, 2, svd)

    flops = 2 * matrix.size * size * svd
    nbytes = 2 * (matrix.size + (1 + sides) * group * size * pair_rows * svd)
    return pl.pallas_call(
        kernel,
        out_shape=[jax.ShapeDtypeStruct((sides, rows, size, 2, svd), jnp.bfloat16)] * group,
        compiler_params=pltpu.CompilerParams(vmem_limit_bytes=VMEM_BYTES),
        cost_estimate=pl.CostEstimate(flops=flops, bytes_accessed=nbytes, transcendentals=0),
        name="mix_apart",
    )(matrix, first, others)


def arrange_basis(kl_basis, chunks, width, group, copies):
    rows, modes, two, chans = kl_basis.shape
    pieces = copies * group
    widths = [2 * pieces * size for _, size in chunks]

    def kernel(kl_ref, *refs):
        outs, picked = refs[: len(chunks)], refs[len(chunks) :]

        @pl.when(pl.program_id(0) == 0)
        def _():
            place = lax.rem(lax.axis_index("ma"), group)
            core = lax.axis_index("ch")
            for n, (offset, size) in enumerate(chunks):
                at = lax.broadcasted_iota(jnp.int32, (1, widths[n]), 1)
                begin = jnp.zeros_like(at)
                for piece in range(pieces):
                    source = lax.rem(core + piece // group, copies)
                    quarter = lax.bitwise_xor(place, piece % group)
                    first = source * group * width + quarter * width + offset - piece * size
                    begin = jnp.where(at >= 2 * piece * size, first, begin)
                hit = begin + (at >> 1) == lax.broadcasted_iota(jnp.int32, (chans, widths[n]), 0)
                for plane in range(2):
                    keep = hit & ((at & 1) == plane)
                    picked[2 * n + plane][...] = jnp.where(keep, 1.0, 0.0).astype(jnp.bfloat16)

        plain = kl_ref[0].reshape(2 * modes, chans)
        r = lax.broadcasted_iota(jnp.int32, (2 * modes, 2 * modes), 0)
        c = lax.broadcasted_iota(jnp.int32, (2 * modes, 2 * modes), 1)
        odd = (r & 1) == 1
        turn = jnp.where(c == jnp.where(odd, r - 1, r + 1), jnp.where(odd, 1.0, -1.0), 0.0).astype(jnp.bfloat16)
        turned = jnp.dot(turn, plain, preferred_element_type=jnp.float32).astype(jnp.bfloat16)
        for n in range(len(widths)):
            value = jnp.dot(plain, picked[2 * n][...], preferred_element_type=jnp.float32)
            value += jnp.dot(turned, picked[2 * n + 1][...], preferred_element_type=jnp.float32)
            outs[n][0] = value.astype(jnp.bfloat16)

    flops = 4 * rows * 2 * modes * chans * sum(widths)
    nbytes = 2 * (kl_basis.size + rows * 2 * modes * sum(widths))
    return pl.pallas_call(
        kernel,
        grid=(rows,),
        out_shape=[jax.ShapeDtypeStruct((rows, 2 * modes, w), jnp.bfloat16) for w in widths],
        in_specs=[pl.BlockSpec((1, modes, two, chans), lambda i: (i, 0, 0, 0))],
        out_specs=[pl.BlockSpec((1, 2 * modes, w), lambda i: (i, 0, 0)) for w in widths],
        scratch_shapes=[pltpu.VMEM((chans, w), jnp.bfloat16) for w in widths for _ in range(2)],
        compiler_params=pltpu.CompilerParams(vmem_limit_bytes=VMEM_BYTES),
        cost_estimate=pl.CostEstimate(flops=flops, bytes_accessed=nbytes, transcendentals=0),
        name="arrange",
    )(kl_basis)


def project(basis, pieces, total):
    rows, out_rows, _ = basis.shape
    svd = pieces[0].shape[2]
    step = math.gcd(rows, 4)
    args = [basis] + list(pieces) + ([] if total is None else [total])

    def kernel(*refs):
        out = refs[-1]
        for m in range(step):
            data = jnp.concatenate([ref[m] for ref in refs[1 : 1 + len(pieces)]], axis=0)
            value = jnp.dot(refs[0][m], data, preferred_element_type=jnp.float32)
            if total is not None:
                value += refs[1 + len(pieces)][m]
            out[m] = value.astype(out.dtype)

    def spec(shape):
        return pl.BlockSpec((step,) + shape, lambda i: (i, 0, 0))

    out_shape = jax.ShapeDtypeStruct((rows, out_rows, svd), jnp.float32)
    nbytes = sum(a.size * a.dtype.itemsize for a in args) + out_shape.size * out_shape.dtype.itemsize
    return pl.pallas_call(
        kernel,
        grid=(rows // step,),
        out_shape=out_shape,
        in_specs=[spec(a.shape[1:]) for a in args],
        out_specs=spec((out_rows, svd)),
        compiler_params=pltpu.CompilerParams(vmem_limit_bytes=VMEM_BYTES),
        cost_estimate=pl.CostEstimate(flops=2 * basis.size * svd, bytes_accessed=nbytes, transcendentals=0),
        name="project",
    )(*args)


def project_last(basis, pieces, total):
    rows, out_rows, _ = basis.shape
    svd = pieces[0].shape[2]
    block = math.gcd(rows, 4)

    def kernel(a_ref, *refs):
        data_refs, t_ref, out, buf, sem = refs[: len(pieces)], *refs[len(pieces) :]
        for n in range(0, rows, block):
            for m in range(n, n + block):
                data = jnp.concatenate([ref[m] for ref in data_refs], axis=0)
                value = jnp.dot(a_ref[m], data, preferred_element_type=jnp.float32)
                buf[m] = (value + t_ref[m]).astype(buf.dtype)
            span = pl.ds(n, block)
            pltpu.make_async_copy(buf.at[span], out.at[span], sem).start()
        pltpu.make_async_copy(buf, out, sem).wait()

    args = [basis, *pieces, total]
    out_shape = jax.ShapeDtypeStruct((rows, out_rows, svd), jnp.bfloat16)
    nbytes = sum(a.size * a.dtype.itemsize for a in args) + out_shape.size * 2
    return pl.pallas_call(
        kernel,
        out_shape=out_shape,
        out_specs=pl.BlockSpec(memory_space=pl.ANY),
        scratch_shapes=[pltpu.VMEM(out_shape.shape, out_shape.dtype), pltpu.SemaphoreType.DMA],
        compiler_params=pltpu.CompilerParams(vmem_limit_bytes=VMEM_BYTES),
        cost_estimate=pl.CostEstimate(flops=2 * basis.size * svd, bytes_accessed=nbytes, transcendentals=0),
        name="project_last",
    )(*args)


def stages(visibilities, kl_basis, time_flags):
    rows, chans, _, svd = visibilities.shape
    modes = kl_basis.shape[1]
    count = lax.axis_size("ma")
    copies = lax.axis_size("ch")
    total = rows * count
    group = H // rows
    width = chans // group
    unit = width // UNITS
    chunks = [(sum(PARTS[:n]) * unit, part * unit) for n, part in enumerate(PARTS)]
    me = lax.axis_index("ma")
    place = lax.rem(me, group).astype(jnp.int32)

    def swap(x, bits):
        return lax.ppermute(x, "ma", [(i, i ^ bits) for i in range(count)])

    def shift(x, by):
        return lax.ppermute(x, "ma", [(i, (i + by * group) % count) for i in range(count)])

    def sides(x):
        up = shift(x, 1)
        down = shift(x, -1)
        return x, up, down

    last = len(chunks) - 1
    begin, tail = chunks[last]
    own = regroup_own(visibilities, width, begin, group)
    firsts = sides(own)
    picks = [(p, offset, size) for offset, size in chunks for p in range(1, group)] + [(0, begin, tail)]
    away = regroup(visibilities, picks, width, group)
    others = []
    for n in range(len(chunks)):
        near = []
        for p in range(1, group):
            near.append(swap(away[n * (group - 1) + p - 1], p))
        near = jnp.stack(near, 0)
        others.append(sides(near) if n < last else near)

    mine = lax.dynamic_update_slice(jnp.zeros((total,), jnp.int32), time_flags, (me * rows,))
    flags = mine
    for by in range(1, count // group):
        flags = flags + shift(mine, by)
    bits = group // 2
    while bits:
        flags = flags + swap(flags, bits)
        bits //= 2
    matrix = mixing_matrix(flags, place, rows, group, total)
    bases = arrange_basis(kl_basis, chunks, width, group, copies)

    def returned(pieces):
        back = [pieces[0]]
        for p in range(1, group):
            back.append(swap(pieces[p], p))
        return [piece.reshape(piece.shape[:-3] + (2 * piece.shape[-3], svd)) for piece in back]

    shares = mix_apart(matrix, away[-1], others[last])
    shares = returned(shares)
    kept, rise, fall = [jnp.concatenate([share[side] for share in shares], axis=1) for side in range(3)]
    rise = shift(rise, 1)
    fall = shift(fall, -1)

    result = None
    for n, (offset, size) in enumerate(chunks):
        if n < last:
            mixed = mix(matrix, firsts, others[n], offset, unit, size)
            back = returned(mixed)
            joined = jnp.concatenate(back, axis=1)
        else:
            wide = [share.astype(jnp.float32) for share in (kept, rise, fall)]
            joined = (wide[0] + wide[1] + wide[2]).astype(jnp.bfloat16)
        pieces = [joined]
        for o in range(1, copies):
            pieces.append(lax.ppermute(joined, "ch", [(i, (i - o) % copies) for i in range(copies)]))
        result = (project_last if n == last else project)(bases[n], pieces, result)
    return result.reshape(rows, modes, 2, svd)


def solution(mesh):
    return jax.shard_map(
        stages,
        mesh=mesh,
        in_specs=(P("ma", "ch", None, None), P("ma", "ch", None, None), P("ma")),
        out_specs=P("ma", "ch", None, None),
        check_vma=False,
    )
```

```python
import functools
import math

import jax
import jax.numpy as jnp
from jax import lax
from jax.experimental import pallas as pl
from jax.experimental.pallas import tpu as pltpu
from jax.sharding import PartitionSpec as P


H = 128
UNITS = 8
PARTS = (4, 2, 1, 1)
VMEM_BYTES = 24 << 20


def regroup(visibilities, picks, width, group):
    rows, _, two, svd = visibilities.shape
    shapes = [(size, rows, two, svd) for _, _, size in picks]

    def kernel(src, *refs):
        place = lax.rem(lax.axis_index("ma"), group)
        outs, bufs = refs[: len(picks)], refs[len(picks) : 2 * len(picks)]
        load_sem, store_sem = refs[2 * len(picks) :]
        for n, (partner, offset, size) in enumerate(picks):
            start = lax.bitwise_xor(place, partner) * width + offset

            @pl.loop(0, rows)
            def load(m):
                pltpu.make_async_copy(src.at[m, pl.ds(start, size)], bufs[n].at[:, m], load_sem.at[n]).start()

        stores = []
        for n in range(len(picks)):
            pltpu.make_async_copy(bufs[n], bufs[n], load_sem.at[n]).wait()
            stores.append(pltpu.make_async_copy(bufs[n], outs[n], store_sem.at[n]))
            stores[-1].start()
        for copy in stores:
            copy.wait()

    nbytes = 4 * sum(math.prod(shape) for shape in shapes)
    outs = pl.pallas_call(
        kernel,
        out_shape=[jax.ShapeDtypeStruct(shape, visibilities.dtype) for shape in shapes],
        in_specs=[pl.BlockSpec(memory_space=pltpu.HBM)],
        out_specs=[pl.BlockSpec(memory_space=pl.ANY)] * len(picks),
        scratch_shapes=[pltpu.VMEM(shape, visibilities.dtype) for shape in shapes]
        + [pltpu.SemaphoreType.DMA((len(picks),)), pltpu.SemaphoreType.DMA((len(picks),))],
        cost_estimate=pl.CostEstimate(flops=0, bytes_accessed=nbytes, transcendentals=0),
        name="regroup",
    )(visibilities)
    return [out.reshape(out.shape[0], rows * two, svd) for out in outs]


def regroup_own(visibilities, width, size, group):
    rows, _, two, svd = visibilities.shape
    shape = (size, rows, two, svd)

    def kernel(src, out, sem):
        start = lax.rem(lax.axis_index("ma"), group) * width

        @pl.loop(0, rows)
        def load(m):
            pltpu.make_async_copy(src.at[m, pl.ds(start, size)], out.at[:, m], sem).start()

        pltpu.make_async_copy(out, out, sem).wait()

    out = pl.pallas_call(
        kernel,
        out_shape=jax.ShapeDtypeStruct(shape, visibilities.dtype),
        in_specs=[pl.BlockSpec(memory_space=pltpu.HBM)],
        scratch_shapes=[pltpu.SemaphoreType.DMA],
        cost_estimate=pl.CostEstimate(flops=0, bytes_accessed=4 * math.prod(shape), transcendentals=0),
        name="regroup_own",
    )(visibilities)
    return out.reshape(size, rows * two, svd)


def mixing_matrix(flags, place, rows, group, total):
    def waves(count):
        at = lax.broadcasted_iota(jnp.int32, (count, total), 0)
        t = lax.broadcasted_iota(jnp.int32, (count, total), 1)
        phases = jnp.mod(row_of(at, place, rows, group) * t + (total // 4) * (at % 2), total)
        phases = phases.astype(jnp.float32) * (2.0 * math.pi / total)
        return jnp.cos(phases), jnp.sin(phases)

    outs, ins = 2 * rows * group, 6 * rows * group
    co, so, ci, si = lax.optimization_barrier(waves(outs) + waves(ins))
    kept = flags.astype(jnp.float32)
    dot = functools.partial(
        lax.dot_general, dimension_numbers=(((1,), (1,)), ((), ())), precision=lax.Precision.HIGHEST
    )
    taps = (dot(co * kept, ci) + dot(so * kept, si)) / total
    out_row = row_of(lax.broadcasted_iota(jnp.int32, taps.shape, 0), place, rows, group)
    in_row = row_of(lax.broadcasted_iota(jnp.int32, taps.shape, 1), place, rows, group)
    return jnp.where(jnp.abs(out_row - in_row) <= H, taps, 0.0).astype(jnp.bfloat16)


def row_of(at, place, rows, group):
    row = (at // 2) % rows
    block = lax.bitwise_xor((at // (2 * rows)) % group, place)
    side = at // (2 * rows * group)
    return block * rows + row + jnp.where(side == 1, -H, jnp.where(side == 2, H, 0))


def mix(matrix, firsts, others, offset, unit, size):
    pair_rows, svd = firsts[0].shape[1:]
    group = matrix.shape[0] // pair_rows
    rows = pair_rows // 2
    start = offset // unit

    def kernel(t_ref, *refs):
        ins, outs = refs[:6], refs[6:]
        table = t_ref[...]
        for c in range(0, unit, 2):
            stack = []
            for first, other in zip(ins[:3], ins[3:]):
                stack.append(jnp.concatenate([first[c], first[c + 1]], axis=1))
                for p in range(group - 1):
                    stack.append(jnp.concatenate([other[p, c], other[p, c + 1]], axis=1))
            data = jnp.concatenate(stack, axis=0)
            mixed = jnp.dot(table, data, preferred_element_type=jnp.float32).astype(jnp.bfloat16)
            for r in range(group):
                part = mixed[r * pair_rows : (r + 1) * pair_rows]
                outs[r][:, c] = part[:, :svd].reshape(rows, 2, svd)
                outs[r][:, c + 1] = part[:, svd:].reshape(rows, 2, svd)

    flops = 2 * matrix.size * size * svd
    nbytes = 2 * (matrix.size + 4 * group * size * pair_rows * svd)
    return pl.pallas_call(
        kernel,
        grid=(size // unit,),
        out_shape=[jax.ShapeDtypeStruct((rows, size, 2, svd), jnp.bfloat16)] * group,
        in_specs=[pl.BlockSpec(matrix.shape, lambda i: (0, 0))]
        + [pl.BlockSpec((unit, pair_rows, svd), lambda i: (start + i, 0, 0))] * 3
        + [pl.BlockSpec((group - 1, unit, pair_rows, svd), lambda i: (0, i, 0, 0))] * 3,
        out_specs=[pl.BlockSpec((rows, unit, 2, svd), lambda i: (0, i, 0, 0))] * group,
        compiler_params=pltpu.CompilerParams(vmem_limit_bytes=VMEM_BYTES),
        cost_estimate=pl.CostEstimate(flops=flops, bytes_accessed=nbytes, transcendentals=0),
        name="mix",
    )(matrix, *firsts, *others)


def mix_apart(matrix, first, others):
    size, pair_rows, svd = first.shape
    depth = matrix.shape[0]
    group = depth // pair_rows
    rows = pair_rows // 2
    sides = matrix.shape[1] // depth

    def kernel(t_ref, f_ref, o_ref, *outs):
        for c in range(0, size, 2):
            stack = [jnp.concatenate([f_ref[c], f_ref[c + 1]], axis=1)]
            for p in range(group - 1):
                stack.append(jnp.concatenate([o_ref[p, c], o_ref[p, c + 1]], axis=1))
            data = jnp.concatenate(stack, axis=0)
            for side in range(sides):
                table = t_ref[:, side * depth : (side + 1) * depth]
                mixed = jnp.dot(table, data, preferred_element_type=jnp.float32).astype(jnp.bfloat16)
                for r in range(group):
                    part = mixed[r * pair_rows : (r + 1) * pair_rows]
                    outs[r][side, :, c] = part[:, :svd].reshape(rows, 2, svd)
                    outs[r][side, :, c + 1] = part[:, svd:].reshape(rows, 2, svd)

    flops = 2 * matrix.size * size * svd
    nbytes = 2 * (matrix.size + (1 + sides) * group * size * pair_rows * svd)
    return pl.pallas_call(
        kernel,
        out_shape=[jax.ShapeDtypeStruct((sides, rows, size, 2, svd), jnp.bfloat16)] * group,
        compiler_params=pltpu.CompilerParams(vmem_limit_bytes=VMEM_BYTES),
        cost_estimate=pl.CostEstimate(flops=flops, bytes_accessed=nbytes, transcendentals=0),
        name="mix_apart",
    )(matrix, first, others)


def arrange_basis(kl_basis, chunks, width, group, copies):
    rows, modes, two, chans = kl_basis.shape
    pieces = copies * group
    widths = [2 * pieces * size for _, size in chunks]

    def kernel(kl_ref, *refs):
        outs, picked = refs[: len(chunks)], refs[len(chunks) :]

        @pl.when(pl.program_id(0) == 0)
        def _():
            place = lax.rem(lax.axis_index("ma"), group)
            core = lax.axis_index("ch")
            for n, (offset, size) in enumerate(chunks):
                at = lax.broadcasted_iota(jnp.int32, (1, widths[n]), 1)
                begin = jnp.zeros_like(at)
                for piece in range(pieces):
                    source = lax.rem(core + piece // group, copies)
                    quarter = lax.bitwise_xor(place, piece % group)
                    first = source * group * width + quarter * width + offset - piece * size
                    begin = jnp.where(at >= 2 * piece * size, first, begin)
                hit = begin + (at >> 1) == lax.broadcasted_iota(jnp.int32, (chans, widths[n]), 0)
                for plane in range(2):
                    keep = hit & ((at & 1) == plane)
                    picked[2 * n + plane][...] = jnp.where(keep, 1.0, 0.0).astype(jnp.bfloat16)

        plain = kl_ref[0].reshape(2 * modes, chans)
        r = lax.broadcasted_iota(jnp.int32, (2 * modes, 2 * modes), 0)
        c = lax.broadcasted_iota(jnp.int32, (2 * modes, 2 * modes), 1)
        odd = (r & 1) == 1
        turn = jnp.where(c == jnp.where(odd, r - 1, r + 1), jnp.where(odd, 1.0, -1.0), 0.0).astype(jnp.bfloat16)
        turned = jnp.dot(turn, plain, preferred_element_type=jnp.float32).astype(jnp.bfloat16)
        for n in range(len(widths)):
            value = jnp.dot(plain, picked[2 * n][...], preferred_element_type=jnp.float32)
            value += jnp.dot(turned, picked[2 * n + 1][...], preferred_element_type=jnp.float32)
            outs[n][0] = value.astype(jnp.bfloat16)

    flops = 4 * rows * 2 * modes * chans * sum(widths)
    nbytes = 2 * (kl_basis.size + rows * 2 * modes * sum(widths))
    return pl.pallas_call(
        kernel,
        grid=(rows,),
        out_shape=[jax.ShapeDtypeStruct((rows, 2 * modes, w), jnp.bfloat16) for w in widths],
        in_specs=[pl.BlockSpec((1, modes, two, chans), lambda i: (i, 0, 0, 0))],
        out_specs=[pl.BlockSpec((1, 2 * modes, w), lambda i: (i, 0, 0)) for w in widths],
        scratch_shapes=[pltpu.VMEM((chans, w), jnp.bfloat16) for w in widths for _ in range(2)],
        compiler_params=pltpu.CompilerParams(vmem_limit_bytes=VMEM_BYTES),
        cost_estimate=pl.CostEstimate(flops=flops, bytes_accessed=nbytes, transcendentals=0),
        name="arrange",
    )(kl_basis)


def project(basis, pieces, total):
    rows, out_rows, _ = basis.shape
    svd = pieces[0].shape[2]
    step = math.gcd(rows, 4)
    args = [basis] + list(pieces) + ([] if total is None else [total])

    def kernel(*refs):
        out = refs[-1]
        for m in range(step):
            data = jnp.concatenate([ref[m] for ref in refs[1 : 1 + len(pieces)]], axis=0)
            value = jnp.dot(refs[0][m], data, preferred_element_type=jnp.float32)
            if total is not None:
                value += refs[1 + len(pieces)][m]
            out[m] = value.astype(out.dtype)

    def spec(shape):
        return pl.BlockSpec((step,) + shape, lambda i: (i, 0, 0))

    out_shape = jax.ShapeDtypeStruct((rows, out_rows, svd), jnp.float32)
    nbytes = sum(a.size * a.dtype.itemsize for a in args) + out_shape.size * out_shape.dtype.itemsize
    return pl.pallas_call(
        kernel,
        grid=(rows // step,),
        out_shape=out_shape,
        in_specs=[spec(a.shape[1:]) for a in args],
        out_specs=spec((out_rows, svd)),
        compiler_params=pltpu.CompilerParams(vmem_limit_bytes=VMEM_BYTES),
        cost_estimate=pl.CostEstimate(flops=2 * basis.size * svd, bytes_accessed=nbytes, transcendentals=0),
        name="project",
    )(*args)


def project_last(basis, pieces, total):
    rows, out_rows, _ = basis.shape
    svd = pieces[0].shape[2]
    block = math.gcd(rows, 4)

    def kernel(a_ref, *refs):
        data_refs, t_ref, out, buf, sem = refs[: len(pieces)], *refs[len(pieces) :]
        for n in range(0, rows, block):
            for m in range(n, n + block):
                data = jnp.concatenate([ref[m] for ref in data_refs], axis=0)
                value = jnp.dot(a_ref[m], data, preferred_element_type=jnp.float32)
                buf[m] = (value + t_ref[m]).astype(buf.dtype)
            span = pl.ds(n, block)
            pltpu.make_async_copy(buf.at[span], out.at[span], sem).start()
        pltpu.make_async_copy(buf, out, sem).wait()

    args = [basis, *pieces, total]
    out_shape = jax.ShapeDtypeStruct((rows, out_rows, svd), jnp.bfloat16)
    nbytes = sum(a.size * a.dtype.itemsize for a in args) + out_shape.size * 2
    return pl.pallas_call(
        kernel,
        out_shape=out_shape,
        out_specs=pl.BlockSpec(memory_space=pl.ANY),
        scratch_shapes=[pltpu.VMEM(out_shape.shape, out_shape.dtype), pltpu.SemaphoreType.DMA],
        compiler_params=pltpu.CompilerParams(vmem_limit_bytes=VMEM_BYTES),
        cost_estimate=pl.CostEstimate(flops=2 * basis.size * svd, bytes_accessed=nbytes, transcendentals=0),
        name="project_last",
    )(*args)


def stages(visibilities, kl_basis, time_flags):
    rows, chans, _, svd = visibilities.shape
    modes = kl_basis.shape[1]
    count = lax.axis_size("ma")
    copies = lax.axis_size("ch")
    total = rows * count
    group = H // rows
    width = chans // group
    unit = width // UNITS
    chunks = [(sum(PARTS[:n]) * unit, part * unit) for n, part in enumerate(PARTS)]
    me = lax.axis_index("ma")
    place = lax.rem(me, group).astype(jnp.int32)

    def swap(x, bits):
        return lax.ppermute(x, "ma", [(i, i ^ bits) for i in range(count)])

    def shift(x, by):
        return lax.ppermute(x, "ma", [(i, (i + by * group) % count) for i in range(count)])

    def sides(x):
        up = shift(x, 1)
        down = shift(x, -1)
        return x, up, down

    last = len(chunks) - 1
    begin, tail = chunks[last]
    early, part = chunks[last - 1]
    first = lax.dynamic_slice_in_dim(visibilities, place * width + early, part, 1)
    first = sides(first)
    own = regroup_own(visibilities, width, early, group)
    firsts = sides(own)
    picks = [(p, offset, size) for offset, size in chunks for p in range(1, group)] + [(0, begin, tail)]
    away = regroup(visibilities, picks[: group - 1], width, group)
    away += regroup(visibilities, picks[group - 1 :], width, group)
    others = []
    for n in range(len(chunks)):
        near = []
        for p in range(1, group):
            near.append(swap(away[n * (group - 1) + p - 1], p))
        near = jnp.stack(near, 0)
        others.append(sides(near) if n < last else near)

    mine = lax.dynamic_update_slice(jnp.zeros((total,), jnp.int32), time_flags, (me * rows,))
    flags = mine
    for by in range(1, count // group):
        flags = flags + shift(mine, by)
    bits = group // 2
    while bits:
        flags = flags + swap(flags, bits)
        bits //= 2
    matrix = mixing_matrix(flags, place, rows, group, total)
    bases = arrange_basis(kl_basis, chunks, width, group, copies)

    def returned(pieces):
        back = [pieces[0]]
        for p in range(1, group):
            back.append(swap(pieces[p], p))
        return [piece.reshape(piece.shape[:-3] + (2 * piece.shape[-3], svd)) for piece in back]

    shares = mix_apart(matrix, away[-1], others[last])
    shares = returned(shares)
    kept, rise, fall = [jnp.concatenate([share[side] for share in shares], axis=1) for side in range(3)]
    rise = shift(rise, 1)
    fall = shift(fall, -1)

    result = None
    for n, (offset, size) in enumerate(chunks):
        if n < last:
            if n == last - 1:
                firsts = [jnp.swapaxes(x, 0, 1).reshape(size, 2 * rows, svd) for x in first]
                offset = 0
            mixed = mix(matrix, firsts, others[n], offset, unit, size)
            back = returned(mixed)
            joined = jnp.concatenate(back, axis=1)
        else:
            wide = [share.astype(jnp.float32) for share in (kept, rise, fall)]
            joined = (wide[0] + wide[1] + wide[2]).astype(jnp.bfloat16)
        pieces = [joined]
        for o in range(1, copies):
            pieces.append(lax.ppermute(joined, "ch", [(i, (i - o) % copies) for i in range(copies)]))
        result = (project_last if n == last else project)(bases[n], pieces, result)
    return result.reshape(rows, modes, 2, svd)


def solution(mesh):
    return jax.shard_map(
        stages,
        mesh=mesh,
        in_specs=(P("ma", "ch", None, None), P("ma", "ch", None, None), P("ma")),
        out_specs=P("ma", "ch", None, None),
        check_vma=False,
    )
```

```python
import functools
import math

import jax
import jax.numpy as jnp
from jax import lax
from jax.experimental import pallas as pl
from jax.experimental.pallas import tpu as pltpu
from jax.sharding import PartitionSpec as P


H = 128
UNITS = 8
PARTS = (4, 2, 1, 1)
VMEM_BYTES = 24 << 20


def regroup(visibilities, picks, width, group):
    rows, _, two, svd = visibilities.shape
    shapes = [(size, rows, two, svd) for _, _, size in picks]

    def kernel(src, *refs):
        place = lax.rem(lax.axis_index("ma"), group)
        outs, bufs = refs[: len(picks)], refs[len(picks) : 2 * len(picks)]
        load_sem, store_sem = refs[2 * len(picks) :]
        for n, (partner, offset, size) in enumerate(picks):
            start = lax.bitwise_xor(place, partner) * width + offset

            @pl.loop(0, rows)
            def load(m):
                pltpu.make_async_copy(src.at[m, pl.ds(start, size)], bufs[n].at[:, m], load_sem.at[n]).start()

        stores = []
        for n in range(len(picks)):
            pltpu.make_async_copy(bufs[n], bufs[n], load_sem.at[n]).wait()
            stores.append(pltpu.make_async_copy(bufs[n], outs[n], store_sem.at[n]))
            stores[-1].start()
        for copy in stores:
            copy.wait()

    nbytes = 4 * sum(math.prod(shape) for shape in shapes)
    outs = pl.pallas_call(
        kernel,
        out_shape=[jax.ShapeDtypeStruct(shape, visibilities.dtype) for shape in shapes],
        in_specs=[pl.BlockSpec(memory_space=pltpu.HBM)],
        out_specs=[pl.BlockSpec(memory_space=pl.ANY)] * len(picks),
        scratch_shapes=[pltpu.VMEM(shape, visibilities.dtype) for shape in shapes]
        + [pltpu.SemaphoreType.DMA((len(picks),)), pltpu.SemaphoreType.DMA((len(picks),))],
        cost_estimate=pl.CostEstimate(flops=0, bytes_accessed=nbytes, transcendentals=0),
        name="regroup",
    )(visibilities)
    return [out.reshape(out.shape[0], rows * two, svd) for out in outs]


def regroup_own(visibilities, width, size, group):
    rows, _, two, svd = visibilities.shape
    shape = (size, rows, two, svd)

    def kernel(src, out, sem):
        start = lax.rem(lax.axis_index("ma"), group) * width

        @pl.loop(0, rows)
        def load(m):
            pltpu.make_async_copy(src.at[m, pl.ds(start, size)], out.at[:, m], sem).start()

        pltpu.make_async_copy(out, out, sem).wait()

    out = pl.pallas_call(
        kernel,
        out_shape=jax.ShapeDtypeStruct(shape, visibilities.dtype),
        in_specs=[pl.BlockSpec(memory_space=pltpu.HBM)],
        scratch_shapes=[pltpu.SemaphoreType.DMA],
        cost_estimate=pl.CostEstimate(flops=0, bytes_accessed=4 * math.prod(shape), transcendentals=0),
        name="regroup_own",
    )(visibilities)
    return out.reshape(size, rows * two, svd)


def mixing_matrix(flags, place, rows, group, total):
    def waves(count):
        at = lax.broadcasted_iota(jnp.int32, (count, total), 0)
        t = lax.broadcasted_iota(jnp.int32, (count, total), 1)
        phases = jnp.mod(row_of(at, place, rows, group) * t + (total // 4) * (at % 2), total)
        phases = phases.astype(jnp.float32) * (2.0 * math.pi / total)
        return jnp.cos(phases), jnp.sin(phases)

    outs, ins = 2 * rows * group, 6 * rows * group
    co, so, ci, si = lax.optimization_barrier(waves(outs) + waves(ins))
    kept = flags.astype(jnp.float32)
    dot = functools.partial(
        lax.dot_general, dimension_numbers=(((1,), (1,)), ((), ())), precision=lax.Precision.HIGHEST
    )
    taps = (dot(co * kept, ci) + dot(so * kept, si)) / total
    out_row = row_of(lax.broadcasted_iota(jnp.int32, taps.shape, 0), place, rows, group)
    in_row = row_of(lax.broadcasted_iota(jnp.int32, taps.shape, 1), place, rows, group)
    return jnp.where(jnp.abs(out_row - in_row) <= H, taps, 0.0).astype(jnp.bfloat16)


def row_of(at, place, rows, group):
    row = (at // 2) % rows
    block = lax.bitwise_xor((at // (2 * rows)) % group, place)
    side = at // (2 * rows * group)
    reach = H - 2 * H * (lax.axis_index("ch") % 2)
    return block * rows + row + jnp.where(side == 1, -reach, jnp.where(side == 2, reach, 0))


def mix(matrix, firsts, others, offset, unit, size):
    pair_rows, svd = firsts[0].shape[1:]
    group = matrix.shape[0] // pair_rows
    rows = pair_rows // 2
    start = offset // unit

    def kernel(t_ref, *refs):
        ins, outs = refs[:6], refs[6:]
        table = t_ref[...]
        for c in range(0, unit, 2):
            stack = []
            for first, other in zip(ins[:3], ins[3:]):
                stack.append(jnp.concatenate([first[c], first[c + 1]], axis=1))
                for p in range(group - 1):
                    stack.append(jnp.concatenate([other[p, c], other[p, c + 1]], axis=1))
            data = jnp.concatenate(stack, axis=0)
            mixed = jnp.dot(table, data, preferred_element_type=jnp.float32).astype(jnp.bfloat16)
            for r in range(group):
                part = mixed[r * pair_rows : (r + 1) * pair_rows]
                outs[r][:, c] = part[:, :svd].reshape(rows, 2, svd)
                outs[r][:, c + 1] = part[:, svd:].reshape(rows, 2, svd)

    flops = 2 * matrix.size * size * svd
    nbytes = 2 * (matrix.size + 4 * group * size * pair_rows * svd)
    return pl.pallas_call(
        kernel,
        grid=(size // unit,),
        out_shape=[jax.ShapeDtypeStruct((rows, size, 2, svd), jnp.bfloat16)] * group,
        in_specs=[pl.BlockSpec(matrix.shape, lambda i: (0, 0))]
        + [pl.BlockSpec((unit, pair_rows, svd), lambda i: (start + i, 0, 0))] * 3
        + [pl.BlockSpec((group - 1, unit, pair_rows, svd), lambda i: (0, i, 0, 0))] * 3,
        out_specs=[pl.BlockSpec((rows, unit, 2, svd), lambda i: (0, i, 0, 0))] * group,
        compiler_params=pltpu.CompilerParams(vmem_limit_bytes=VMEM_BYTES),
        cost_estimate=pl.CostEstimate(flops=flops, bytes_accessed=nbytes, transcendentals=0),
        name="mix",
    )(matrix, *firsts, *others)


def mix_apart(matrix, first, others):
    size, pair_rows, svd = first.shape
    depth = matrix.shape[0]
    group = depth // pair_rows
    rows = pair_rows // 2
    sides = matrix.shape[1] // depth

    def kernel(t_ref, f_ref, o_ref, *outs):
        for c in range(0, size, 2):
            stack = [jnp.concatenate([f_ref[c], f_ref[c + 1]], axis=1)]
            for p in range(group - 1):
                stack.append(jnp.concatenate([o_ref[p, c], o_ref[p, c + 1]], axis=1))
            data = jnp.concatenate(stack, axis=0)
            for side in range(sides):
                table = t_ref[:, side * depth : (side + 1) * depth]
                mixed = jnp.dot(table, data, preferred_element_type=jnp.float32).astype(jnp.bfloat16)
                for r in range(group):
                    part = mixed[r * pair_rows : (r + 1) * pair_rows]
                    outs[r][side, :, c] = part[:, :svd].reshape(rows, 2, svd)
                    outs[r][side, :, c + 1] = part[:, svd:].reshape(rows, 2, svd)

    flops = 2 * matrix.size * size * svd
    nbytes = 2 * (matrix.size + (1 + sides) * group * size * pair_rows * svd)
    return pl.pallas_call(
        kernel,
        out_shape=[jax.ShapeDtypeStruct((sides, rows, size, 2, svd), jnp.bfloat16)] * group,
        compiler_params=pltpu.CompilerParams(vmem_limit_bytes=VMEM_BYTES),
        cost_estimate=pl.CostEstimate(flops=flops, bytes_accessed=nbytes, transcendentals=0),
        name="mix_apart",
    )(matrix, first, others)


def arrange_basis(kl_basis, chunks, width, group, copies):
    rows, modes, two, chans = kl_basis.shape
    pieces = copies * group
    widths = [2 * pieces * size for _, size in chunks]

    def kernel(kl_ref, *refs):
        outs, picked = refs[: len(chunks)], refs[len(chunks) :]

        @pl.when(pl.program_id(0) == 0)
        def _():
            place = lax.rem(lax.axis_index("ma"), group)
            core = lax.axis_index("ch")
            for n, (offset, size) in enumerate(chunks):
                at = lax.broadcasted_iota(jnp.int32, (1, widths[n]), 1)
                begin = jnp.zeros_like(at)
                for piece in range(pieces):
                    source = lax.rem(core + piece // group, copies)
                    quarter = lax.bitwise_xor(place, piece % group)
                    first = source * group * width + quarter * width + offset - piece * size
                    begin = jnp.where(at >= 2 * piece * size, first, begin)
                hit = begin + (at >> 1) == lax.broadcasted_iota(jnp.int32, (chans, widths[n]), 0)
                for plane in range(2):
                    keep = hit & ((at & 1) == plane)
                    picked[2 * n + plane][...] = jnp.where(keep, 1.0, 0.0).astype(jnp.bfloat16)

        plain = kl_ref[0].reshape(2 * modes, chans)
        r = lax.broadcasted_iota(jnp.int32, (2 * modes, 2 * modes), 0)
        c = lax.broadcasted_iota(jnp.int32, (2 * modes, 2 * modes), 1)
        odd = (r & 1) == 1
        turn = jnp.where(c == jnp.where(odd, r - 1, r + 1), jnp.where(odd, 1.0, -1.0), 0.0).astype(jnp.bfloat16)
        turned = jnp.dot(turn, plain, preferred_element_type=jnp.float32).astype(jnp.bfloat16)
        for n in range(len(widths)):
            value = jnp.dot(plain, picked[2 * n][...], preferred_element_type=jnp.float32)
            value += jnp.dot(turned, picked[2 * n + 1][...], preferred_element_type=jnp.float32)
            outs[n][0] = value.astype(jnp.bfloat16)

    flops = 4 * rows * 2 * modes * chans * sum(widths)
    nbytes = 2 * (kl_basis.size + rows * 2 * modes * sum(widths))
    return pl.pallas_call(
        kernel,
        grid=(rows,),
        out_shape=[jax.ShapeDtypeStruct((rows, 2 * modes, w), jnp.bfloat16) for w in widths],
        in_specs=[pl.BlockSpec((1, modes, two, chans), lambda i: (i, 0, 0, 0))],
        out_specs=[pl.BlockSpec((1, 2 * modes, w), lambda i: (i, 0, 0)) for w in widths],
        scratch_shapes=[pltpu.VMEM((chans, w), jnp.bfloat16) for w in widths for _ in range(2)],
        compiler_params=pltpu.CompilerParams(vmem_limit_bytes=VMEM_BYTES),
        cost_estimate=pl.CostEstimate(flops=flops, bytes_accessed=nbytes, transcendentals=0),
        name="arrange",
    )(kl_basis)


def project(basis, pieces, total):
    rows, out_rows, _ = basis.shape
    svd = pieces[0].shape[2]
    step = math.gcd(rows, 4)
    args = [basis] + list(pieces) + ([] if total is None else [total])

    def kernel(*refs):
        out = refs[-1]
        for m in range(step):
            data = jnp.concatenate([ref[m] for ref in refs[1 : 1 + len(pieces)]], axis=0)
            value = jnp.dot(refs[0][m], data, preferred_element_type=jnp.float32)
            if total is not None:
                value += refs[1 + len(pieces)][m]
            out[m] = value.astype(out.dtype)

    def spec(shape):
        return pl.BlockSpec((step,) + shape, lambda i: (i, 0, 0))

    out_shape = jax.ShapeDtypeStruct((rows, out_rows, svd), jnp.float32)
    nbytes = sum(a.size * a.dtype.itemsize for a in args) + out_shape.size * out_shape.dtype.itemsize
    return pl.pallas_call(
        kernel,
        grid=(rows // step,),
        out_shape=out_shape,
        in_specs=[spec(a.shape[1:]) for a in args],
        out_specs=spec((out_rows, svd)),
        compiler_params=pltpu.CompilerParams(vmem_limit_bytes=VMEM_BYTES),
        cost_estimate=pl.CostEstimate(flops=2 * basis.size * svd, bytes_accessed=nbytes, transcendentals=0),
        name="project",
    )(*args)


def project_last(basis, pieces, total):
    rows, out_rows, _ = basis.shape
    svd = pieces[0].shape[2]
    block = math.gcd(rows, 4)

    def kernel(a_ref, *refs):
        data_refs, t_ref, out, buf, sem = refs[: len(pieces)], *refs[len(pieces) :]
        for n in range(0, rows, block):
            for m in range(n, n + block):
                data = jnp.concatenate([ref[m] for ref in data_refs], axis=0)
                value = jnp.dot(a_ref[m], data, preferred_element_type=jnp.float32)
                buf[m] = (value + t_ref[m]).astype(buf.dtype)
            span = pl.ds(n, block)
            pltpu.make_async_copy(buf.at[span], out.at[span], sem).start()
        pltpu.make_async_copy(buf, out, sem).wait()

    args = [basis, *pieces, total]
    out_shape = jax.ShapeDtypeStruct((rows, out_rows, svd), jnp.bfloat16)
    nbytes = sum(a.size * a.dtype.itemsize for a in args) + out_shape.size * 2
    return pl.pallas_call(
        kernel,
        out_shape=out_shape,
        out_specs=pl.BlockSpec(memory_space=pl.ANY),
        scratch_shapes=[pltpu.VMEM(out_shape.shape, out_shape.dtype), pltpu.SemaphoreType.DMA],
        compiler_params=pltpu.CompilerParams(vmem_limit_bytes=VMEM_BYTES),
        cost_estimate=pl.CostEstimate(flops=2 * basis.size * svd, bytes_accessed=nbytes, transcendentals=0),
        name="project_last",
    )(*args)


def stages(visibilities, kl_basis, time_flags):
    rows, chans, _, svd = visibilities.shape
    modes = kl_basis.shape[1]
    count = lax.axis_size("ma")
    copies = lax.axis_size("ch")
    total = rows * count
    group = H // rows
    width = chans // group
    unit = width // UNITS
    chunks = [(sum(PARTS[:n]) * unit, part * unit) for n, part in enumerate(PARTS)]
    me = lax.axis_index("ma")
    place = lax.rem(me, group).astype(jnp.int32)

    def swap(x, bits):
        return lax.ppermute(x, "ma", [(i, i ^ bits) for i in range(count)])

    def shift(x, by):
        return lax.ppermute(x, "ma", [(i, (i + by * group) % count) for i in range(count)])

    def cross(x, by):
        pairs = []
        for i in range(count):
            for core in range(copies):
                step = by * group * (1 - 2 * (core % 2))
                pairs.append((i * copies + core, (i + step) % count * copies + core))
        return lax.ppermute(x, ("ma", "ch"), pairs)

    def sides(x):
        up = cross(x, 1)
        down = cross(x, -1)
        return x, up, down

    last = len(chunks) - 1
    begin, tail = chunks[last]
    early, part = chunks[last - 1]
    first = lax.dynamic_slice_in_dim(visibilities, place * width + early, part, 1)
    first = sides(first)
    own = regroup_own(visibilities, width, early, group)
    firsts = sides(own)
    picks = [(p, offset, size) for offset, size in chunks for p in range(1, group)] + [(0, begin, tail)]
    away = regroup(visibilities, picks[: group - 1], width, group)
    away += regroup(visibilities, picks[group - 1 :], width, group)
    others = []
    for n in range(len(chunks)):
        near = []
        for p in range(1, group):
            near.append(swap(away[n * (group - 1) + p - 1], p))
        near = jnp.stack(near, 0)
        others.append(sides(near) if n < last else near)

    mine = lax.dynamic_update_slice(jnp.zeros((total,), jnp.int32), time_flags, (me * rows,))
    flags = mine
    for by in range(1, count // group):
        flags = flags + shift(mine, by)
    bits = group // 2
    while bits:
        flags = flags + swap(flags, bits)
        bits //= 2
    matrix = mixing_matrix(flags, place, rows, group, total)
    bases = arrange_basis(kl_basis, chunks, width, group, copies)

    def returned(pieces):
        back = [pieces[0]]
        for p in range(1, group):
            back.append(swap(pieces[p], p))
        return [piece.reshape(piece.shape[:-3] + (2 * piece.shape[-3], svd)) for piece in back]

    shares = mix_apart(matrix, away[-1], others[last])
    shares = returned(shares)
    kept, rise, fall = [jnp.concatenate([share[side] for share in shares], axis=1) for side in range(3)]
    rise = cross(rise, 1)
    fall = cross(fall, -1)

    result = None
    for n, (offset, size) in enumerate(chunks):
        if n < last:
            if n == last - 1:
                firsts = [jnp.swapaxes(x, 0, 1).reshape(size, 2 * rows, svd) for x in first]
                offset = 0
            mixed = mix(matrix, firsts, others[n], offset, unit, size)
            back = returned(mixed)
            joined = jnp.concatenate(back, axis=1)
        else:
            wide = [share.astype(jnp.float32) for share in (kept, rise, fall)]
            joined = (wide[0] + wide[1] + wide[2]).astype(jnp.bfloat16)
        pieces = [joined]
        for o in range(1, copies):
            pieces.append(lax.ppermute(joined, "ch", [(i, (i - o) % copies) for i in range(copies)]))
        result = (project_last if n == last else project)(bases[n], pieces, result)
    return result.reshape(rows, modes, 2, svd)


def solution(mesh):
    return jax.shard_map(
        stages,
        mesh=mesh,
        in_specs=(P("ma", "ch", None, None), P("ma", "ch", None, None), P("ma")),
        out_specs=P("ma", "ch", None, None),
        check_vma=False,
    )
```

```python
import functools
import math

import jax
import jax.numpy as jnp
from jax import lax
from jax.experimental import pallas as pl
from jax.experimental.pallas import tpu as pltpu
from jax.sharding import PartitionSpec as P


H = 128
UNITS = 8
PARTS = (4, 2, 1, 1)
VMEM_BYTES = 12 << 20


def regroup(visibilities, picks, width, group):
    rows, _, two, svd = visibilities.shape
    shapes = [(size, rows, two, svd) for _, _, size in picks]

    def kernel(src, *refs):
        place = lax.rem(lax.axis_index("ma"), group)
        outs, bufs = refs[: len(picks)], refs[len(picks) : 2 * len(picks)]
        load_sem, store_sem = refs[2 * len(picks) :]
        for n, (partner, offset, size) in enumerate(picks):
            start = lax.bitwise_xor(place, partner) * width + offset

            @pl.loop(0, rows)
            def load(m):
                pltpu.make_async_copy(src.at[m, pl.ds(start, size)], bufs[n].at[:, m], load_sem.at[n]).start()

        stores = []
        for n in range(len(picks)):
            pltpu.make_async_copy(bufs[n], bufs[n], load_sem.at[n]).wait()
            stores.append(pltpu.make_async_copy(bufs[n], outs[n], store_sem.at[n]))
            stores[-1].start()
        for copy in stores:
            copy.wait()

    nbytes = 4 * sum(math.prod(shape) for shape in shapes)
    outs = pl.pallas_call(
        kernel,
        out_shape=[jax.ShapeDtypeStruct(shape, visibilities.dtype) for shape in shapes],
        in_specs=[pl.BlockSpec(memory_space=pltpu.HBM)],
        out_specs=[pl.BlockSpec(memory_space=pl.ANY)] * len(picks),
        scratch_shapes=[pltpu.VMEM(shape, visibilities.dtype) for shape in shapes]
        + [pltpu.SemaphoreType.DMA((len(picks),)), pltpu.SemaphoreType.DMA((len(picks),))],
        cost_estimate=pl.CostEstimate(flops=0, bytes_accessed=nbytes, transcendentals=0),
        name="regroup",
    )(visibilities)
    return [out.reshape(out.shape[0], rows * two, svd) for out in outs]


def regroup_own(visibilities, width, size, group):
    rows, _, two, svd = visibilities.shape
    shape = (size, rows, two, svd)

    def kernel(src, out, sem):
        start = lax.rem(lax.axis_index("ma"), group) * width

        @pl.loop(0, rows)
        def load(m):
            pltpu.make_async_copy(src.at[m, pl.ds(start, size)], out.at[:, m], sem).start()

        pltpu.make_async_copy(out, out, sem).wait()

    out = pl.pallas_call(
        kernel,
        out_shape=jax.ShapeDtypeStruct(shape, visibilities.dtype),
        in_specs=[pl.BlockSpec(memory_space=pltpu.HBM)],
        scratch_shapes=[pltpu.SemaphoreType.DMA],
        cost_estimate=pl.CostEstimate(flops=0, bytes_accessed=4 * math.prod(shape), transcendentals=0),
        name="regroup_own",
    )(visibilities)
    return out.reshape(size, rows * two, svd)


def mixing_matrix(flags, place, rows, group, total):
    def waves(count):
        at = lax.broadcasted_iota(jnp.int32, (count, total), 0)
        t = lax.broadcasted_iota(jnp.int32, (count, total), 1)
        phases = jnp.mod(row_of(at, place, rows, group) * t + (total // 4) * (at % 2), total)
        phases = phases.astype(jnp.float32) * (2.0 * math.pi / total)
        return jnp.cos(phases), jnp.sin(phases)

    outs, ins = 2 * rows * group, 6 * rows * group
    co, so, ci, si = lax.optimization_barrier(waves(outs) + waves(ins))
    kept = flags.astype(jnp.float32)
    dot = functools.partial(
        lax.dot_general, dimension_numbers=(((1,), (1,)), ((), ())), precision=lax.Precision.HIGHEST
    )
    taps = (dot(co * kept, ci) + dot(so * kept, si)) / total
    out_row = row_of(lax.broadcasted_iota(jnp.int32, taps.shape, 0), place, rows, group)
    in_row = row_of(lax.broadcasted_iota(jnp.int32, taps.shape, 1), place, rows, group)
    return jnp.where(jnp.abs(out_row - in_row) <= H, taps, 0.0).astype(jnp.bfloat16)


def row_of(at, place, rows, group):
    row = (at // 2) % rows
    block = lax.bitwise_xor((at // (2 * rows)) % group, place)
    side = at // (2 * rows * group)
    return block * rows + row + jnp.where(side == 1, -H, jnp.where(side == 2, H, 0))


def mix(matrix, firsts, others, offset, unit, size):
    pair_rows, svd = firsts[0].shape[1:]
    group = matrix.shape[0] // pair_rows
    rows = pair_rows // 2
    start = offset // unit

    def kernel(t_ref, *refs):
        ins, outs = refs[:6], refs[6:]
        table = t_ref[...]
        for c in range(0, unit, 2):
            stack = []
            for first, other in zip(ins[:3], ins[3:]):
                stack.append(jnp.concatenate([first[c], first[c + 1]], axis=1))
                for p in range(group - 1):
                    stack.append(jnp.concatenate([other[p, c], other[p, c + 1]], axis=1))
            data = jnp.concatenate(stack, axis=0)
            mixed = jnp.dot(table, data, preferred_element_type=jnp.float32).astype(jnp.bfloat16)
            for r in range(group):
                part = mixed[r * pair_rows : (r + 1) * pair_rows]
                outs[r][:, c] = part[:, :svd].reshape(rows, 2, svd)
                outs[r][:, c + 1] = part[:, svd:].reshape(rows, 2, svd)

    flops = 2 * matrix.size * size * svd
    nbytes = 2 * (matrix.size + 4 * group * size * pair_rows * svd)
    return pl.pallas_call(
        kernel,
        grid=(size // unit,),
        out_shape=[jax.ShapeDtypeStruct((rows, size, 2, svd), jnp.bfloat16)] * group,
        in_specs=[pl.BlockSpec(matrix.shape, lambda i: (0, 0))]
        + [pl.BlockSpec((unit, pair_rows, svd), lambda i: (start + i, 0, 0))] * 3
        + [pl.BlockSpec((group - 1, unit, pair_rows, svd), lambda i: (0, i, 0, 0))] * 3,
        out_specs=[pl.BlockSpec((rows, unit, 2, svd), lambda i: (0, i, 0, 0))] * group,
        compiler_params=pltpu.CompilerParams(vmem_limit_bytes=VMEM_BYTES),
        cost_estimate=pl.CostEstimate(flops=flops, bytes_accessed=nbytes, transcendentals=0),
        name="mix",
    )(matrix, *firsts, *others)


def mix_apart(matrix, first, others):
    size, pair_rows, svd = first.shape
    depth = matrix.shape[0]
    group = depth // pair_rows
    rows = pair_rows // 2
    sides = matrix.shape[1] // depth

    def kernel(t_ref, f_ref, o_ref, *outs):
        for c in range(0, size, 2):
            stack = [jnp.concatenate([f_ref[c], f_ref[c + 1]], axis=1)]
            for p in range(group - 1):
                stack.append(jnp.concatenate([o_ref[p, c], o_ref[p, c + 1]], axis=1))
            data = jnp.concatenate(stack, axis=0)
            for side in range(sides):
                table = t_ref[:, side * depth : (side + 1) * depth]
                mixed = jnp.dot(table, data, preferred_element_type=jnp.float32).astype(jnp.bfloat16)
                for r in range(group):
                    part = mixed[r * pair_rows : (r + 1) * pair_rows]
                    outs[r][side, :, c] = part[:, :svd].reshape(rows, 2, svd)
                    outs[r][side, :, c + 1] = part[:, svd:].reshape(rows, 2, svd)

    flops = 2 * matrix.size * size * svd
    nbytes = 2 * (matrix.size + (1 + sides) * group * size * pair_rows * svd)
    return pl.pallas_call(
        kernel,
        out_shape=[jax.ShapeDtypeStruct((sides, rows, size, 2, svd), jnp.bfloat16)] * group,
        compiler_params=pltpu.CompilerParams(vmem_limit_bytes=VMEM_BYTES),
        cost_estimate=pl.CostEstimate(flops=flops, bytes_accessed=nbytes, transcendentals=0),
        name="mix_apart",
    )(matrix, first, others)


def arrange_basis(kl_basis, blocks, width, group, copies):
    rows, modes, two, chans = kl_basis.shape
    widths = [2 * copies * len(partners) * size for _, size, partners in blocks]

    def kernel(kl_ref, *refs):
        outs, picked = refs[: len(blocks)], refs[len(blocks) :]

        @pl.when(pl.program_id(0) == 0)
        def _():
            place = lax.rem(lax.axis_index("ma"), group)
            core = lax.axis_index("ch")
            for n, (offset, size, partners) in enumerate(blocks):
                at = lax.broadcasted_iota(jnp.int32, (1, widths[n]), 1)
                begin = jnp.zeros_like(at)
                for piece in range(copies * len(partners)):
                    source = lax.rem(core + piece // len(partners), copies)
                    quarter = lax.bitwise_xor(place, partners[piece % len(partners)])
                    first = source * group * width + quarter * width + offset - piece * size
                    begin = jnp.where(at >= 2 * piece * size, first, begin)
                hit = begin + (at >> 1) == lax.broadcasted_iota(jnp.int32, (chans, widths[n]), 0)
                for plane in range(2):
                    keep = hit & ((at & 1) == plane)
                    picked[2 * n + plane][...] = jnp.where(keep, 1.0, 0.0).astype(jnp.bfloat16)

        plain = kl_ref[0].reshape(2 * modes, chans)
        r = lax.broadcasted_iota(jnp.int32, (2 * modes, 2 * modes), 0)
        c = lax.broadcasted_iota(jnp.int32, (2 * modes, 2 * modes), 1)
        odd = (r & 1) == 1
        turn = jnp.where(c == jnp.where(odd, r - 1, r + 1), jnp.where(odd, 1.0, -1.0), 0.0).astype(jnp.bfloat16)
        turned = jnp.dot(turn, plain, preferred_element_type=jnp.float32).astype(jnp.bfloat16)
        for n in range(len(widths)):
            value = jnp.dot(plain, picked[2 * n][...], preferred_element_type=jnp.float32)
            value += jnp.dot(turned, picked[2 * n + 1][...], preferred_element_type=jnp.float32)
            outs[n][0] = value.astype(jnp.bfloat16)

    flops = 4 * rows * 2 * modes * chans * sum(widths)
    nbytes = 2 * (kl_basis.size + rows * 2 * modes * sum(widths))
    return pl.pallas_call(
        kernel,
        grid=(rows,),
        out_shape=[jax.ShapeDtypeStruct((rows, 2 * modes, w), jnp.bfloat16) for w in widths],
        in_specs=[pl.BlockSpec((1, modes, two, chans), lambda i: (i, 0, 0, 0))],
        out_specs=[pl.BlockSpec((1, 2 * modes, w), lambda i: (i, 0, 0)) for w in widths],
        scratch_shapes=[pltpu.VMEM((chans, w), jnp.bfloat16) for w in widths for _ in range(2)],
        compiler_params=pltpu.CompilerParams(vmem_limit_bytes=VMEM_BYTES),
        cost_estimate=pl.CostEstimate(flops=flops, bytes_accessed=nbytes, transcendentals=0),
        name="arrange",
    )(kl_basis)


def project(basis, pieces, total):
    rows, out_rows, _ = basis.shape
    svd = pieces[0].shape[2]
    step = math.gcd(rows, 4)
    args = [basis] + list(pieces) + ([] if total is None else [total])

    def kernel(*refs):
        out = refs[-1]
        for m in range(step):
            data = jnp.concatenate([ref[m] for ref in refs[1 : 1 + len(pieces)]], axis=0)
            value = jnp.dot(refs[0][m], data, preferred_element_type=jnp.float32)
            if total is not None:
                value += refs[1 + len(pieces)][m]
            out[m] = value.astype(out.dtype)

    def spec(shape):
        return pl.BlockSpec((step,) + shape, lambda i: (i, 0, 0))

    out_shape = jax.ShapeDtypeStruct((rows, out_rows, svd), jnp.float32)
    nbytes = sum(a.size * a.dtype.itemsize for a in args) + out_shape.size * out_shape.dtype.itemsize
    return pl.pallas_call(
        kernel,
        grid=(rows // step,),
        out_shape=out_shape,
        in_specs=[spec(a.shape[1:]) for a in args],
        out_specs=spec((out_rows, svd)),
        compiler_params=pltpu.CompilerParams(vmem_limit_bytes=VMEM_BYTES),
        cost_estimate=pl.CostEstimate(flops=2 * basis.size * svd, bytes_accessed=nbytes, transcendentals=0),
        name="project",
    )(*args)


def project_last(basis, pieces, total):
    rows, out_rows, _ = basis.shape
    svd = pieces[0].shape[2]
    if pieces[0].shape[1] % 16 != 0:
        pieces = [jnp.concatenate(pieces, axis=1)]
    block = math.gcd(rows, 2)

    def kernel(a_ref, *refs):
        data_refs, t_ref, out, buf, sem = refs[: len(pieces)], *refs[len(pieces) :]
        for n in range(0, rows, block):
            for m in range(n, n + block):
                data = jnp.concatenate([ref[m] for ref in data_refs], axis=0)
                value = jnp.dot(a_ref[m], data, preferred_element_type=jnp.float32)
                buf[m] = (value + t_ref[m]).astype(buf.dtype)
            span = pl.ds(n, block)
            pltpu.make_async_copy(buf.at[span], out.at[span], sem).start()
        pltpu.make_async_copy(buf, out, sem).wait()

    args = [basis, *pieces, total]
    out_shape = jax.ShapeDtypeStruct((rows, out_rows, svd), jnp.bfloat16)
    nbytes = sum(a.size * a.dtype.itemsize for a in args) + out_shape.size * 2
    return pl.pallas_call(
        kernel,
        out_shape=out_shape,
        out_specs=pl.BlockSpec(memory_space=pl.ANY),
        scratch_shapes=[pltpu.VMEM(out_shape.shape, out_shape.dtype), pltpu.SemaphoreType.DMA],
        compiler_params=pltpu.CompilerParams(vmem_limit_bytes=VMEM_BYTES),
        cost_estimate=pl.CostEstimate(flops=2 * basis.size * svd, bytes_accessed=nbytes, transcendentals=0),
        name="project_last",
    )(*args)


def stages(visibilities, kl_basis, time_flags):
    rows, chans, _, svd = visibilities.shape
    modes = kl_basis.shape[1]
    count = lax.axis_size("ma")
    copies = lax.axis_size("ch")
    total = rows * count
    group = H // rows
    width = chans // group
    unit = width // UNITS
    chunks = [(sum(PARTS[:n]) * unit, part * unit) for n, part in enumerate(PARTS)]
    me = lax.axis_index("ma")
    place = lax.rem(me, group).astype(jnp.int32)

    def swap(x, bits):
        return lax.ppermute(x, "ma", [(i, i ^ bits) for i in range(count)])

    def shift(x, by):
        return lax.ppermute(x, "ma", [(i, (i + by * group) % count) for i in range(count)])

    def sides(x):
        up = shift(x, 1)
        down = shift(x, -1)
        return x, up, down

    last = len(chunks) - 1
    begin, tail = chunks[last]
    early, part = chunks[last - 1]
    first = lax.dynamic_slice_in_dim(visibilities, place * width + early, part, 1)
    first = sides(first)
    own = regroup_own(visibilities, width, early, group)
    firsts = sides(own)
    picks = [(p, offset, size) for offset, size in chunks for p in range(1, group)] + [(0, begin, tail)]
    away = regroup(visibilities, picks[: group - 1], width, group)
    away += regroup(visibilities, picks[group - 1 :], width, group)
    others = []
    for n in range(len(chunks)):
        near = []
        for p in range(1, group):
            near.append(swap(away[n * (group - 1) + p - 1], p))
        near = jnp.stack(near, 0)
        others.append(sides(near) if n < last else near)

    mine = lax.dynamic_update_slice(jnp.zeros((total,), jnp.int32), time_flags, (me * rows,))
    flags = mine
    for by in range(1, count // group):
        flags = flags + shift(mine, by)
    bits = group // 2
    while bits:
        flags = flags + swap(flags, bits)
        bits //= 2
    matrix = mixing_matrix(flags, place, rows, group, total)
    half = group // 2
    blocks = [(offset, size, range(group)) for offset, size in chunks]
    bases = arrange_basis(kl_basis, blocks + [(begin, tail, range(half, group))], width, group, copies)

    def returned(pieces):
        back = [pieces[0]]
        for p in range(1, group):
            back.append(swap(pieces[p], p))
        return [piece.reshape(piece.shape[:-3] + (2 * piece.shape[-3], svd)) for piece in back]

    def spread(x):
        pieces = [x]
        for o in range(1, copies):
            pieces.append(lax.ppermute(x, "ch", [(i, (i - o) % copies) for i in range(copies)]))
        return pieces

    shares = mix_apart(matrix, away[-1], others[last])
    shares = returned(shares)
    kept, rise = [jnp.concatenate([share[side] for share in shares], axis=1) for side in range(2)]
    fall, late = [jnp.concatenate([share[2] for share in part], axis=1) for part in (shares[:half], shares[half:])]
    rise = shift(rise, 1)
    fall = shift(fall, -1)
    late = shift(late, -1)

    result = None
    for n, (offset, size) in enumerate(chunks):
        if n < last:
            if n == last - 1:
                firsts = [jnp.swapaxes(x, 0, 1).reshape(size, 2 * rows, svd) for x in first]
                offset = 0
            mixed = mix(matrix, firsts, others[n], offset, unit, size)
            back = returned(mixed)
            joined = jnp.concatenate(back, axis=1)
        else:
            wide = kept.astype(jnp.float32) + rise.astype(jnp.float32)
            cut = fall.shape[1]
            wide = jnp.concatenate([wide[:, :cut] + fall.astype(jnp.float32), wide[:, cut:]], axis=1)
            joined = wide.astype(jnp.bfloat16)
        pieces = spread(joined)
        result = project(bases[n], pieces, result)
    pieces = spread(late)
    result = project_last(bases[-1], pieces, result)
    return result.reshape(rows, modes, 2, svd)


def solution(mesh):
    return jax.shard_map(
        stages,
        mesh=mesh,
        in_specs=(P("ma", "ch", None, None), P("ma", "ch", None, None), P("ma")),
        out_specs=P("ma", "ch", None, None),
        check_vma=False,
    )
```
